128 devices in a mesh: seq: 8 (over z, core), head: 16 (over x, y).
Axes of the slice: x: 4, y: 4, z: 4, core: 2. Of those that a mesh axis runs over, the one named last changes fastest.
Arguments:
- query_raw: bfloat16 [8192, 8192], P('seq', 'head'), may hold values from -12 to 12
- key_raw: bfloat16 [8192, 8192], P('seq', 'head'), may hold values from -6 to 6
- value_raw: bfloat16 [8192, 8192], P('seq', 'head'), may hold values from -6 to 6
- query_gain: float32 [8192], P('head'), may hold values from 0.1 to 1.9
- log_decay: float32 [64, 8192], P('head', 'seq'), may hold values from -1.5 to 0
- out_grad: bfloat16 [8192, 8192], P('seq', 'head'), may hold values from -0.75 to 0.75
Outputs:
- query_raw_grad: bfloat16 [8192, 8192], P(('seq', 'head'))
- key_raw_grad: bfloat16 [8192, 8192], P(('seq', 'head'))
- value_raw_grad: bfloat16 [8192, 8192], P(('seq', 'head'))
The draws below stay inside these ranges and needn't reach their ends.
All inputs are finite; a program needn't handle non-finite values.
Results may differ from the reference program's by a relative error of at most 0.0021.
Values may be sent and summed in bfloat16 or wider, within the bound.
No kernel may reach another device: no remote copies, remote signals or barrier semaphores. Data moves between devices by JAX's collectives and lax.ppermute only.
A program may use at most 128 MiB of HBM per device.

```python
import math
import jax
import jax.numpy as jnp
from jax import lax

H = 64
HD = 128
D = 8192
TOKENS = 8192


def draw_query_raw(key, part):
    streams = jax.random.split(jax.random.fold_in(key, 11), 3)
    entries = jax.random.truncated_normal(streams[0], -4.0, 4.0, (TOKENS, D), jnp.float32)
    row_scale = 0.1 * jnp.exp(jax.random.uniform(streams[1], (TOKENS, 1), jnp.float32, 0.0, math.log(10.0)))
    column = lax.broadcasted_iota(jnp.int32, (D,), 0).astype(jnp.float32)
    col_scale = 0.1 * jnp.exp(jax.random.uniform(streams[2], (D,), jnp.float32, 0.0, math.log(10.0)))
    col_scale = col_scale * jnp.exp(math.log(3.0) * column / D)
    return (entries * row_scale * col_scale[None, :]).astype(jnp.bfloat16)


def draw_log_decay(key, part):
    streams = jax.random.split(jax.random.fold_in(key, 23), 4)
    share = 0.5
    quick = jax.random.bernoulli(streams[0], share, (H, 1))
    initial_amount = jnp.where(quick, 1.0 / 40.0, 0.3 / TOKENS)
    multiplier = jnp.exp(jax.random.uniform(streams[1], (H, TOKENS), jnp.float32, -math.log(2.0), math.log(2.0)))
    location_sequence = jax.random.randint(streams[2], (H, 2), 0, TOKENS)
    objective_numbers = jax.random.uniform(streams[3], (H, 2), jnp.float32, 0.2, 0.5)
    element_slot = lax.broadcasted_iota(jnp.int32, (H, 2, TOKENS), 2)
    cluster_sets = jnp.sum(jnp.where(element_slot == location_sequence[:, :, None], jnp.log1p(-objective_numbers)[:, :, None], 0.0), axis=1)
    return -initial_amount * multiplier + cluster_sets


def levels(key, extent, cuts, smallest, largest):
    def one(position, parts):
        steps = jax.random.uniform(jax.random.fold_in(jax.random.fold_in(key, 6), position), (parts,), jnp.float32, smallest / len(cuts), largest / len(cuts))
        return jnp.repeat(jnp.exp(steps), extent[position] // parts).reshape((-1,) + (1,) * (len(extent) - position - 1))

    level = one(*cuts[0])
    for cut in cuts[1:]:
        level = level * one(*cut)
    return level


def centred(key, shape, spread, reach, shards=(), dtype=jnp.bfloat16):
    gain = levels(key, shape, shards, -0.22, 0.18) if shards else 1.0
    result = jax.random.normal(key, shape, jnp.float32) * spread * gain
    return jnp.minimum(jnp.maximum(result, -reach), reach).astype(dtype)


def setup_inputs(seed: int = 0) -> dict:
    seeds = jax.random.split(jax.random.key(seed), 7)
    return {
        "query_raw": draw_query_raw(jax.random.fold_in(seeds[6], 71), 0),
        "key_raw": centred(seeds[1], (TOKENS, D), 1.0, 6.0, ((0, 8), (1, 16))),
        "value_raw": centred(seeds[2], (TOKENS, D), 1.0, 6.0, ((0, 8), (1, 16))),
        "query_gain": jnp.clip(1.0 + 0.18 * jax.random.normal(seeds[3], (D,), jnp.float32), 0.1, 1.9),
        "log_decay": draw_log_decay(jax.random.fold_in(seeds[6], 71), 0),
        "out_grad": centred(seeds[5], (TOKENS, D), 0.05, 0.75, ((0, 8), (1, 16))),
    }


epsilon = 1e-06

def recurrence(queries, keys, values, decay):
    block_len = math.gcd(TOKENS, 32)
    count = TOKENS // block_len

    def token_step(state_matrix, inputs):
        query_vector, key, value, rate = inputs
        recall_score = jnp.einsum('dzt,dz->dt', state_matrix, key)
        update = value - rate[:, None] * recall_score
        state_matrix = rate[:, None, None] * state_matrix + 2.0 * key[:, :, None] * update[:, None, :]
        return (state_matrix, jnp.einsum('dzt,dz->dt', state_matrix, query_vector))

    @jax.checkpoint
    def block_step(state_matrix, block):
        return lax.scan(token_step, state_matrix, block)

    def split(array):
        return array.reshape((count, block_len) + array.shape[1:])
    start = jnp.zeros((H, HD, HD), jnp.float32)
    _, outputs = lax.scan(block_step, start, (split(queries), split(keys), split(values), split(decay)))
    return outputs.reshape(TOKENS, H, HD)

def reference(query_raw, key_raw, value_raw, query_gain, log_decay, out_grad):
    raw_query = query_raw.astype(jnp.float32)
    inv_rms = 1.0 / jnp.sqrt(lax.optimization_barrier(jnp.mean(raw_query * raw_query, axis=1, keepdims=True)) + epsilon)
    normed = raw_query * inv_rms
    scale = HD ** (-0.5)
    queries = (normed * query_gain * scale).reshape(TOKENS, H, HD)
    raw_key = key_raw.astype(jnp.float32).reshape(TOKENS, H, HD)
    key_scale = 1.0 / jnp.sqrt(lax.optimization_barrier(jnp.sum(raw_key * raw_key, axis=2, keepdims=True)) + epsilon)
    keys = raw_key * key_scale
    values = value_raw.astype(jnp.float32).reshape(TOKENS, H, HD)
    decay = jnp.exp(log_decay).T

    def forward(query_part, key_part, value_part):
        return recurrence(query_part, key_part, value_part, decay)
    head_out, pullback = jax.vjp(forward, queries, keys, values)
    query_grad, key_grad, value_grad = pullback(out_grad.astype(jnp.float32).reshape(TOKENS, H, HD))
    scaled = query_grad.reshape(TOKENS, D) * query_gain * scale
    correction = lax.optimization_barrier(jnp.mean(scaled * normed, axis=1, keepdims=True))
    query_raw_grad = (inv_rms * (scaled - normed * correction)).astype(jnp.bfloat16)
    key_raw_grad = key_scale * (key_grad - keys * lax.optimization_barrier(jnp.sum(keys * key_grad, axis=2, keepdims=True)))
    key_raw_grad = key_raw_grad.reshape(TOKENS, D).astype(jnp.bfloat16)
    value_raw_grad = value_grad.reshape(TOKENS, D).astype(jnp.bfloat16)
    return (query_raw_grad, key_raw_grad, value_raw_grad)
```

```python
import functools

import jax
import jax.numpy as jnp
from jax import lax
from jax.experimental import pallas as pl
from jax.experimental.pallas import tpu as pltpu
from jax.sharding import Mesh
from jax.sharding import PartitionSpec as P

D = 8192
C = 128
PAIR = 2
HEAD = ("head_0", "head_1")
SEQ = ("seq_0", "seq_1")
SEQ_HEAD = ("seq_0", "seq_1", "head_0", "head_1")
EPS = 1e-06
SCALE = C ** (-0.5)

f32 = jnp.float32
bf16 = jnp.bfloat16


def halves(x):
    high = x.astype(bf16)
    return high, (x - high.astype(f32)).astype(bf16)


def nn(a, b):
    return lax.dot_general(a, b, (((1,), (0,)), ((), ())), preferred_element_type=f32)


def nt(a, b):
    return lax.dot_general(a, b, (((1,), (1,)), ((), ())), preferred_element_type=f32)


def mul3(form, a, b):
    return form(a[0], b[0]) + (form(a[0], b[1]) + form(a[1], b[0]))


def mul_left(form, a, b):
    return form(a[0], b) + form(a[1], b)


def mul_right(form, a, b):
    return form(a, b[0]) + form(a, b[1])


def iotas():
    return (
        lax.broadcasted_iota(jnp.int32, (C, C), 0),
        lax.broadcasted_iota(jnp.int32, (C, C), 1),
    )


def columns_of(rows):
    missing = C - rows.shape[0]
    return jnp.concatenate([rows, jnp.zeros((missing, C), f32)], axis=0).T


def tile(ref, b, h):
    return ref[b * C : (b + 1) * C, h * C : (h + 1) * C]


def prep_keys(heads, steps, key, value, decay, inv, weight, trans, shift, cols, rows, send, whole, offset):
    step = pl.program_id(0)
    units = [(b, h) for b in range(PAIR) for h in range(heads)]
    count = len(units)
    row, col = iotas()
    lane = lax.broadcasted_iota(jnp.int32, (C, C), 1)

    @pl.when(step == 0)
    def _():
        eye = jnp.where(row == col, 1.0, 0.0)
        for h in range(heads):
            whole[h] = eye
            offset[h] = jnp.zeros((C, C), f32)

    upto = jnp.where(row <= col, 1.0, 0.0)
    logs = jnp.concatenate([decay[:, b * C : (b + 1) * C] for b in range(PAIR)], axis=0)
    cumul_rows = jnp.dot(logs, upto, precision=lax.Precision.HIGHEST, preferred_element_type=f32)
    cumul_cols = columns_of(cumul_rows)

    raw = [tile(key, b, h) for b, h in units]
    scale_cols = []
    gathered = jnp.zeros((C, C), f32)
    for u in range(count):
        wide = raw[u].astype(f32)
        scale_cols.append(lax.rsqrt(jnp.sum(wide * wide, axis=1, keepdims=True) + EPS))
        gathered = jnp.where(lane == u, scale_cols[u], gathered)
    scale_rows = gathered.T

    rows[0, :count] = cumul_rows
    rows[0, count:] = scale_rows[:count]
    for b in range(PAIR):
        packed = jnp.zeros((C, C), f32)
        for h in range(heads):
            u = b * heads + h
            packed = jnp.where(lane == h, cumul_cols[:, u : u + 1], packed)
            packed = jnp.where(lane == heads + h, scale_cols[u], packed)
        cols[b * C : (b + 1) * C] = packed

    g_col = [cumul_cols[:, u : u + 1] for u in range(count)]
    g_row = [cumul_rows[u : u + 1] for u in range(count)]
    s_row = [scale_rows[u : u + 1] for u in range(count)]
    last = [g_row[u][:, C - 1 :] for u in range(count)]

    lower = []
    for u in range(count):
        gram = nt(raw[u], raw[u])
        decayed = jnp.exp(jnp.where(row > col, g_col[u] - g_row[u], 0.0))
        lower.append(
            jnp.where(row > col, 2.0 * decayed * (scale_cols[u] * s_row[u]) * gram, 0.0)
        )

    apart = row ^ col
    result = [
        jnp.where(row == col, 1.0, 0.0) - jnp.where(apart == 1, lower[u], 0.0) for u in range(count)
    ]
    size = 2
    while size < C:
        here = (apart >= size) & (apart < 2 * size)
        split = [halves(x) for x in result]
        below = [halves(jnp.where(here, lower[u], 0.0)) for u in range(count)]
        inner = [halves(mul3(nn, below[u], split[u])) for u in range(count)]
        result = [result[u] - mul3(nn, split[u], inner[u]) for u in range(count)]
        size *= 2

    for u in range(count):
        inv[u] = result[u]
    split = [halves(x) for x in result]
    scaled = []
    for u in range(count):
        end = jnp.exp(last[u] - g_row[u])
        turned = tile(value, *units[u]).T
        amount = mul_right(nt, turned, split[u]) * (2.0 * end * s_row[u])
        shift[u] = mul_left(nn, halves(amount), raw[u])
        start = jnp.exp(g_row[u]) * s_row[u]
        scaled.append(mul_left(nn, halves(result[u] * start), raw[u]))
        weight[u] = scaled[u]
    for u in range(count):
        end = jnp.exp(last[u] - g_col[u]) * (2.0 * scale_cols[u])
        drop = mul_right(nn, raw[u].T, halves(scaled[u] * end))
        trans[u] = jnp.where(row == col, jnp.exp(last[u]), 0.0) - drop

    for b in range(PAIR):
        for h in range(heads):
            u = b * heads + h
            step_map = halves(trans[u])
            whole[h] = mul3(nn, step_map, halves(whole[h]))
            offset[h] = mul3(nt, halves(offset[h]), step_map) + shift[u]

    @pl.when(step == steps - 1)
    def _():
        half = C // 2
        for h in range(heads):
            for part in range(2):
                send[2 * h + part, :C] = whole[h]
                send[2 * h + part, C:] = offset[h, part * half : (part + 1) * half]


def prep_queries(heads, query, key, grad, gain, sums, weight, trans, cols, rows, inner, adjoint, norm_cols, norm_rows, send, total):
    step = pl.program_id(0)
    units = [(b, h) for b in range(PAIR) for h in range(heads)]
    count = len(units)
    row, col = iotas()

    @pl.when(step == 0)
    def _():
        for h in range(heads):
            total[h] = jnp.zeros((C, C), f32)

    squares = jnp.sum(sums[...], axis=0, keepdims=True)
    norm = lax.rsqrt(squares * (1.0 / D) + EPS)
    per_block = jnp.concatenate([norm[:, b * C : (b + 1) * C] for b in range(PAIR)], axis=0)
    n_cols = columns_of(per_block)
    norm_rows[0] = jnp.concatenate([per_block, jnp.zeros((8 - PAIR, C), f32)], axis=0)
    for b in range(PAIR):
        norm_cols[b * C : (b + 1) * C] = jnp.broadcast_to(n_cols[:, b : b + 1], (C, C))

    scaled_query, mixing = [], []
    for u, (b, h) in enumerate(units):
        here = cols[b * C : (b + 1) * C]
        g_col = here[:, h : h + 1]
        g_row = rows[0, u : u + 1]
        s_row = rows[0, count + u : count + u + 1]
        n_col = n_cols[:, b : b + 1]
        wide = tile(query, b, h).astype(f32) * (gain[:, h * C : (h + 1) * C] * SCALE)
        decayed = jnp.exp(jnp.where(row >= col, g_col - g_row, 0.0))
        scores = mul_left(nt, halves(wide), tile(key, b, h))
        mixing.append(
            halves(jnp.where(row >= col, 2.0 * decayed * (n_col * s_row) * scores, 0.0))
        )
        scaled_query.append(halves(wide * (jnp.exp(g_col) * n_col)))
    turned = [tile(grad, b, h).T for b, h in units]
    for u in range(count):
        inner[u] = mul_right(nn, turned[u], mixing[u])
    for u in range(count):
        adjoint[u] = mul_right(nn, turned[u], scaled_query[u]) - mul3(
            nn, halves(inner[u]), halves(weight[u])
        )
    for b in reversed(range(PAIR)):
        for h in range(heads):
            u = b * heads + h
            total[h] = mul3(nn, halves(total[h]), halves(trans[u])) + adjoint[u]

    half = C // 2
    for h in range(heads):
        for part in range(2):
            send[2 * h + part] = total[h, part * half : (part + 1) * half]


def scan_states(received, out):
    count = received.shape[0]
    state = jnp.zeros(out.shape[1:], f32)
    for k in range(count):
        out[k] = state
        if k < count - 1:
            state = mul3(nt, halves(state), halves(received[k, :C])) + received[k, C:]


def scan_adjoints(maps, received, out):
    count = received.shape[0]
    state = jnp.zeros(out.shape[1:], f32)
    for k in reversed(range(count)):
        out[k] = state
        if k:
            state = mul3(nn, halves(state), halves(maps[k, :C])) + received[k]


def query_grads(heads, query, key, value, grad, gain, incoming, inv, weight, trans, shift, cols, rows, norm_cols, scaled, fresh, starts, part, state):
    step = pl.program_id(0)
    units = [(b, h) for b in range(PAIR) for h in range(heads)]
    count = len(units)
    row, col = iotas()
    lane = lax.broadcasted_iota(jnp.int32, (C, C), 1)

    @pl.when(step == 0)
    def _():
        state[...] = incoming[...]

    for b in range(PAIR):
        for h in range(heads):
            u = b * heads + h
            starts[u] = state[h]
            state[h] = mul3(nt, halves(state[h]), halves(trans[u])) + shift[u]
    begin = [halves(starts[u]) for u in range(count)]
    amounts = []
    for u, (b, h) in enumerate(units):
        amount = mul_left(nn, halves(inv[u]), tile(value, b, h)) - mul3(
            nt, halves(weight[u]), begin[u]
        )
        fresh[u] = amount
        amounts.append(halves(amount))
    cross = [mul_right(nt, tile(grad, b, h), amounts[u]) for u, (b, h) in enumerate(units)]
    sums = [jnp.zeros((C, 1), f32) for _ in range(PAIR)]
    for u, (b, h) in enumerate(units):
        here = cols[b * C : (b + 1) * C]
        g_col = here[:, h : h + 1]
        g_row = rows[0, u : u + 1]
        s_row = rows[0, count + u : count + u + 1]
        decayed = jnp.exp(jnp.where(row >= col, g_col - g_row, 0.0))
        mixed = jnp.where(row >= col, 2.0 * decayed * s_row * cross[u], 0.0)
        result = mul_left(nn, halves(mixed), tile(key, b, h)) + jnp.exp(g_col) * mul_right(
            nn, tile(grad, b, h), begin[u]
        )
        result = result * (gain[:, h * C : (h + 1) * C] * SCALE)
        scaled[b * C : (b + 1) * C, h * C : (h + 1) * C] = result
        sums[b] = sums[b] + jnp.sum(result * tile(query, b, h).astype(f32), axis=1, keepdims=True)
    for b in range(PAIR):
        full = sums[b] * norm_cols[b * C : (b + 1) * C]
        part[:, b * C : (b + 1) * C] = full.T[: part.shape[0]]


def finish_queries(query, scaled, norm_cols, sums, out):
    total = jnp.sum(sums[...], axis=0, keepdims=True) * (1.0 / D)
    blocks = total.shape[1] // C
    per_block = jnp.concatenate([total[:, b * C : (b + 1) * C] for b in range(blocks)], axis=0)
    corrections = columns_of(per_block)
    for b in range(blocks):
        part = slice(b * C, (b + 1) * C)
        norm = norm_cols[part][:, :1]
        normed = query[part].astype(f32) * norm
        out[part] = (norm * (scaled[part] - normed * corrections[:, b : b + 1])).astype(bf16)


def key_grads(heads, query, key, grad, gain, outgoing, inv, trans, adjoint, inner, fresh, starts, cols, rows, norm_rows, key_out, value_out, state):
    step = pl.program_id(0)
    units = [(b, h) for b in range(PAIR) for h in range(heads)]
    count = len(units)
    row, col = iotas()

    @pl.when(step == 0)
    def _():
        state[...] = outgoing[...]

    ends = [None] * count
    for b in reversed(range(PAIR)):
        for h in range(heads):
            u = b * heads + h
            ends[u] = halves(state[h])
            state[h] = mul3(nn, ends[u], halves(trans[u])) + adjoint[u]
    g_row = [rows[0, u : u + 1] for u in range(count)]
    s_row = [rows[0, count + u : count + u + 1] for u in range(count)]
    keys = [tile(key, b, h) for b, h in units]
    amounts = [halves(fresh[u]) for u in range(count)]
    turned = []
    for u in range(count):
        end = jnp.exp(g_row[u][:, C - 1 :] - g_row[u]) * (2.0 * s_row[u])
        turned.append(halves(inner[u] + mul_left(nt, ends[u], keys[u]) * end))
    results = [mul3(nn, turned[u], halves(inv[u])).T for u in range(count)]
    for u, (b, h) in enumerate(units):
        value_out[b * C : (b + 1) * C, h * C : (h + 1) * C] = results[u].astype(bf16)
    results = [halves(x) for x in results]
    against = [mul3(nt, results[u], amounts[u]) for u in range(count)]
    across = [mul_left(nt, amounts[u], tile(grad, b, h)) for u, (b, h) in enumerate(units)]
    for u, (b, h) in enumerate(units):
        here = cols[b * C : (b + 1) * C]
        g_col = here[:, h : h + 1]
        s_col = here[:, heads + h : heads + h + 1]
        n_row = norm_rows[0, b : b + 1]
        below = jnp.exp(jnp.where(row > col, g_col - g_row[u], 0.0))
        pulled = jnp.where(row > col, -2.0 * below * against[u], 0.0)
        both = (pulled + pulled.T) * s_row[u]
        above = jnp.exp(jnp.where(row <= col, g_row[u] - g_col, 0.0))
        mixed = jnp.where(row <= col, 2.0 * above * n_row * across[u], 0.0)
        total = mul_left(nn, halves(both), keys[u])
        total += mul_left(nn, halves(mixed), tile(query, b, h)) * (
            gain[:, h * C : (h + 1) * C] * SCALE
        )
        total -= jnp.exp(g_col) * mul3(nn, results[u], halves(starts[u]))
        end = 2.0 * jnp.exp(g_row[u][:, C - 1 :] - g_col)
        total += end * mul3(nn, amounts[u], ends[u])
        unit = keys[u].astype(f32) * s_col
        along = jnp.sum(unit * total, axis=1, keepdims=True)
        key_out[b * C : (b + 1) * C, h * C : (h + 1) * C] = (
            s_col * (total - unit * along)
        ).astype(bf16)


def from_everyone(value, axis):
    length = lax.axis_size(axis)
    return lax.all_to_all(
        jnp.broadcast_to(value[None], (length, *value.shape)), axis, 0, 0, tiled=True
    )


def per_device(query_raw, key_raw, value_raw, query_gain, log_decay, out_grad):
    rows, width = query_raw.shape
    heads = log_decay.shape[0]
    blocks = rows // C
    steps = blocks // PAIR
    count = PAIR * heads
    tokens = PAIR * C
    group = lax.axis_size(HEAD)
    chain = lax.axis_size(SEQ)
    gain = query_gain.reshape(1, width)
    shape = jax.ShapeDtypeStruct

    def forward(*block):
        return pl.BlockSpec(block, lambda i: (i,) + (0,) * (len(block) - 1))

    def backward(*block):
        return pl.BlockSpec(block, lambda i: (steps - 1 - i,) + (0,) * (len(block) - 1))

    def fixed(*block):
        return pl.BlockSpec(block, lambda i: (0,) * len(block))

    def lanes(order, *block):
        return pl.BlockSpec(block, lambda i: (0, order(i)))

    def ahead(i):
        return i

    def back(i):
        return steps - 1 - i

    matrices = shape((blocks * heads, C, C), f32)
    matrix = (count, C, C)
    carry = pltpu.VMEM((heads, C, C), f32)

    wide = query_raw.astype(f32)
    squares = from_everyone(jnp.sum(wide * wide, axis=1)[None], HEAD).reshape(group, rows)

    inv, weight, trans, shift, cols, row_info, send = pl.pallas_call(
        functools.partial(prep_keys, heads, steps),
        grid=(steps,),
        in_specs=[forward(tokens, width), forward(tokens, width), lanes(ahead, heads, tokens)],
        out_specs=[forward(*matrix)] * 4
        + [forward(tokens, C), forward(1, 2 * count, C), fixed(2 * heads, C + C // 2, C)],
        out_shape=[matrices] * 4
        + [
            shape((rows, C), f32),
            shape((steps, 2 * count, C), f32),
            shape((2 * heads, C + C // 2, C), f32),
        ],
        scratch_shapes=[carry, carry],
        name="prep_keys",
    )(key_raw, value_raw, log_decay)
    maps = lax.all_to_all(send, SEQ, 0, 0, tiled=True)

    inner, adjoint, norm_cols, norm_rows, send_back = pl.pallas_call(
        functools.partial(prep_queries, heads),
        grid=(steps,),
        in_specs=[
            backward(tokens, width),
            backward(tokens, width),
            backward(tokens, width),
            fixed(1, width),
            lanes(back, group, tokens),
            backward(*matrix),
            backward(*matrix),
            backward(tokens, C),
            backward(1, 2 * count, C),
        ],
        out_specs=[
            backward(*matrix),
            backward(*matrix),
            backward(tokens, C),
            backward(1, 8, C),
            fixed(2 * heads, C // 2, C),
        ],
        out_shape=[
            matrices,
            matrices,
            shape((rows, C), f32),
            shape((steps, 8, C), f32),
            shape((2 * heads, C // 2, C), f32),
        ],
        scratch_shapes=[carry],
        name="prep_queries",
    )(query_raw, key_raw, out_grad, gain, squares, weight, trans, cols, row_info)
    late = lax.all_to_all(send_back, SEQ, 0, 0, tiled=True)

    pieces = shape((chain, C // 2, C), f32)
    incoming = lax.all_to_all(
        pl.pallas_call(scan_states, out_shape=pieces, name="scan_states")(maps),
        SEQ,
        0,
        0,
        tiled=True,
    ).reshape(heads, C, C)
    outgoing = lax.all_to_all(
        pl.pallas_call(scan_adjoints, out_shape=pieces, name="scan_adjoints")(maps, late),
        SEQ,
        0,
        0,
        tiled=True,
    ).reshape(heads, C, C)

    scaled, fresh, starts, part = pl.pallas_call(
        functools.partial(query_grads, heads),
        grid=(steps,),
        in_specs=[forward(tokens, width)] * 4
        + [fixed(1, width), fixed(heads, C, C)]
        + [forward(*matrix)] * 4
        + [forward(tokens, C), forward(1, 2 * count, C), forward(tokens, C)],
        out_specs=[
            forward(tokens, width),
            forward(*matrix),
            forward(*matrix),
            lanes(ahead, 8, tokens),
        ],
        out_shape=[shape((rows, width), f32), matrices, matrices, shape((8, rows), f32)],
        scratch_shapes=[carry],
        name="query_grads",
    )(
        query_raw, key_raw, value_raw, out_grad, gain, incoming,
        inv, weight, trans, shift, cols, row_info, norm_cols,
    )
    corrections = from_everyone(part[:1], HEAD).reshape(group, rows)

    key_raw_grad, value_raw_grad = pl.pallas_call(
        functools.partial(key_grads, heads),
        grid=(steps,),
        in_specs=[backward(tokens, width)] * 3
        + [fixed(1, width), fixed(heads, C, C)]
        + [backward(*matrix)] * 6
        + [backward(tokens, C), backward(1, 2 * count, C), backward(1, 8, C)],
        out_specs=[backward(tokens, width)] * 2,
        out_shape=[shape((rows, width), bf16)] * 2,
        scratch_shapes=[carry],
        name="key_grads",
    )(
        query_raw, key_raw, out_grad, gain, outgoing,
        inv, trans, adjoint, inner, fresh, starts, cols, row_info, norm_rows,
    )

    query_raw_grad = pl.pallas_call(
        finish_queries,
        grid=(steps,),
        in_specs=[
            forward(tokens, width),
            forward(tokens, width),
            forward(tokens, C),
            lanes(ahead, group, tokens),
        ],
        out_specs=forward(tokens, width),
        out_shape=shape((rows, width), bf16),
        name="finish_queries",
    )(query_raw, scaled, norm_cols, corrections)

    def owned(array):
        return lax.all_to_all(array, HEAD, split_axis=0, concat_axis=1, tiled=True)

    return owned(query_raw_grad), owned(key_raw_grad), owned(value_raw_grad)


def solution(mesh):
    split = Mesh(mesh.devices.reshape(4, 2, 4, 4), ("seq_0", "seq_1", "head_0", "head_1"))
    return jax.shard_map(
        per_device,
        mesh=split,
        in_specs=(P(SEQ, HEAD), P(SEQ, HEAD), P(SEQ, HEAD), P(HEAD), P(HEAD, SEQ), P(SEQ, HEAD)),
        out_specs=(P(SEQ_HEAD, None), P(SEQ_HEAD, None), P(SEQ_HEAD, None)),
        check_vma=False,
    )
```

```python
import functools

import jax
import jax.numpy as jnp
from jax import lax
from jax.experimental import pallas as pl
from jax.experimental.pallas import tpu as pltpu
from jax.sharding import Mesh
from jax.sharding import PartitionSpec as P

D = 8192
C = 128
PAIRS = (2, 2, 2, 2, 2)
HEAD = ("head_0", "head_1")
SEQ = ("seq_0", "seq_1")
SEQ_HEAD = ("seq_0", "seq_1", "head_0", "head_1")
EPS = 1e-06
SCALE = C ** (-0.5)

f32 = jnp.float32
bf16 = jnp.bfloat16


def halves(x):
    high = x.astype(bf16)
    return high, (x - high.astype(f32)).astype(bf16)


def nn(a, b):
    return lax.dot_general(a, b, (((1,), (0,)), ((), ())), preferred_element_type=f32)


def nt(a, b):
    return lax.dot_general(a, b, (((1,), (1,)), ((), ())), preferred_element_type=f32)


def mul3(form, a, b):
    return form(a[0], b[0]) + (form(a[0], b[1]) + form(a[1], b[0]))


def mul_left(form, a, b):
    return form(a[0], b) + form(a[1], b)


def mul_right(form, a, b):
    return form(a, b[0]) + form(a, b[1])


def iotas():
    return (
        lax.broadcasted_iota(jnp.int32, (C, C), 0),
        lax.broadcasted_iota(jnp.int32, (C, C), 1),
    )


def columns_of(rows):
    missing = C - rows.shape[0]
    return jnp.concatenate([rows, jnp.zeros((missing, C), f32)], axis=0).T


def tile(ref, b, h):
    return ref[b * C : (b + 1) * C, h * C : (h + 1) * C]


def square_sums(query, out):
    blocks = query.shape[0] // C
    ones = jnp.full((out.shape[0], query.shape[1]), 1.0, bf16)
    wide = query[...].astype(f32)
    sums = mul_right(nt, ones, halves(wide * wide))
    for b in range(blocks):
        out[:, b] = sums[:, b * C : (b + 1) * C]


def all_units(pair, heads):
    return [(b, h) for b in range(pair) for h in range(heads)]


def prep_keys(pair, heads, steps, key, value, decay, inv, weight, trans, shift, cols, rows, send, whole, offset):
    step = pl.program_id(0)
    units = all_units(pair, heads)
    count = len(units)
    row, col = iotas()

    @pl.when(step == 0)
    def _():
        eye = jnp.where(row == col, 1.0, 0.0)
        for h in range(heads):
            whole[h] = eye
            offset[h] = jnp.zeros((C, C), f32)

    upto = jnp.where(row <= col, 1.0, 0.0)
    logs = jnp.concatenate([decay[:, b * C : (b + 1) * C] for b in range(pair)], axis=0)
    cumul_rows = jnp.dot(logs, upto, precision=lax.Precision.HIGHEST, preferred_element_type=f32)
    cumul_cols = columns_of(cumul_rows)

    raw = [tile(key, b, h) for b, h in units]
    scale_cols = []
    gathered = jnp.zeros((C, C), f32)
    for u in range(count):
        wide = raw[u].astype(f32)
        scale_cols.append(lax.rsqrt(jnp.sum(wide * wide, axis=1, keepdims=True) + EPS))
        gathered = jnp.where(col == u, scale_cols[u], gathered)
    scale_rows = gathered.T

    for b in range(pair):
        mine = slice(b * heads, (b + 1) * heads)
        rows[b] = jnp.concatenate([cumul_rows[mine], scale_rows[mine]], axis=0)
        packed = jnp.zeros((C, C), f32)
        for h in range(heads):
            u = b * heads + h
            packed = jnp.where(col == h, cumul_cols[:, u : u + 1], packed)
            packed = jnp.where(col == heads + h, scale_cols[u], packed)
        cols[b * C : (b + 1) * C] = packed

    g_col = [cumul_cols[:, u : u + 1] for u in range(count)]
    g_row = [cumul_rows[u : u + 1] for u in range(count)]
    s_row = [scale_rows[u : u + 1] for u in range(count)]
    last = [g_row[u][:, C - 1 :] for u in range(count)]

    lower = []
    for u in range(count):
        gram = nt(raw[u], raw[u])
        decayed = jnp.exp(jnp.where(row > col, g_col[u] - g_row[u], 0.0))
        lower.append(
            jnp.where(row > col, 2.0 * decayed * (scale_cols[u] * s_row[u]) * gram, 0.0)
        )

    apart = row ^ col
    result = [
        jnp.where(row == col, 1.0, 0.0) - jnp.where(apart == 1, lower[u], 0.0) for u in range(count)
    ]
    size = 2
    while size < C:
        here = (apart >= size) & (apart < 2 * size)
        split = [halves(x) for x in result]
        below = [halves(jnp.where(here, lower[u], 0.0)) for u in range(count)]
        inner = [halves(mul3(nn, below[u], split[u])) for u in range(count)]
        result = [result[u] - mul3(nn, split[u], inner[u]) for u in range(count)]
        size *= 2

    split = [halves(x) for x in result]
    scaled, moved = [], []
    for u, (b, h) in enumerate(units):
        inv[b, h] = result[u]
        end = jnp.exp(last[u] - g_row[u])
        turned = tile(value, b, h).T
        amount = mul_right(nt, turned, split[u]) * (2.0 * end * s_row[u])
        moved.append(mul_left(nn, halves(amount), raw[u]))
        shift[b, h] = moved[u]
        start = jnp.exp(g_row[u]) * s_row[u]
        scaled.append(mul_left(nn, halves(result[u] * start), raw[u]))
        weight[b, h] = scaled[u]
    maps = []
    for u, (b, h) in enumerate(units):
        end = jnp.exp(last[u] - g_col[u]) * (2.0 * scale_cols[u])
        drop = mul_right(nn, raw[u].T, halves(scaled[u] * end))
        maps.append(jnp.where(row == col, jnp.exp(last[u]), 0.0) - drop)
        trans[b, h] = maps[u]

    for b in range(pair):
        for h in range(heads):
            u = b * heads + h
            step_map = halves(maps[u])
            whole[h] = mul3(nn, step_map, halves(whole[h]))
            offset[h] = mul3(nt, halves(offset[h]), step_map) + moved[u]

    @pl.when(step == steps - 1)
    def _():
        half = C // 2
        for h in range(heads):
            for part in range(2):
                send[2 * h + part, :C] = whole[h]
                send[2 * h + part, C:] = offset[h, part * half : (part + 1) * half]


def prep_queries(pair, heads, steps, query, key, grad, gain, sums, weight, trans, cols, rows, inner, adjoint, norm_cols, norm_rows, send, total, norms):
    step = pl.program_id(0)
    units = all_units(pair, heads)
    count = len(units)
    row, col = iotas()

    @pl.when(step == 0)
    def _():
        for h in range(heads):
            total[h] = jnp.zeros((C, C), f32)
        norms[...] = lax.rsqrt(jnp.sum(sums[...], axis=0) * (1.0 / D) + EPS)

    first = (steps - 1 - step) * pair
    n_rows = [norms[pl.ds(first + b, 1)] for b in range(pair)]
    n_cols = columns_of(jnp.concatenate(n_rows, axis=0))
    for b in range(pair):
        norm_rows[b] = jnp.broadcast_to(n_rows[b], (8, C))
        norm_cols[b * C : (b + 1) * C] = jnp.broadcast_to(n_cols[:, b : b + 1], (C, C))

    scaled_query, mixing = [], []
    for u, (b, h) in enumerate(units):
        here = cols[b * C : (b + 1) * C]
        g_col = here[:, h : h + 1]
        g_row = rows[b, h : h + 1]
        s_row = rows[b, heads + h : heads + h + 1]
        n_col = n_cols[:, b : b + 1]
        wide = tile(query, b, h).astype(f32) * (gain[:, h * C : (h + 1) * C] * SCALE)
        decayed = jnp.exp(jnp.where(row >= col, g_col - g_row, 0.0))
        scores = mul_left(nt, halves(wide), tile(key, b, h))
        mixing.append(
            halves(jnp.where(row >= col, 2.0 * decayed * (n_col * s_row) * scores, 0.0))
        )
        scaled_query.append(halves(wide * (jnp.exp(g_col) * n_col)))
    turned = [tile(grad, b, h).T for b, h in units]
    mixed = [mul_right(nn, turned[u], mixing[u]) for u in range(count)]
    terms = []
    for u, (b, h) in enumerate(units):
        inner[b, h] = mixed[u]
        terms.append(
            mul_right(nn, turned[u], scaled_query[u])
            - mul3(nn, halves(mixed[u]), halves(weight[b, h]))
        )
        adjoint[b, h] = terms[u]
    for b in reversed(range(pair)):
        for h in range(heads):
            u = b * heads + h
            total[h] = mul3(nn, halves(total[h]), halves(trans[b, h])) + terms[u]

    half = C // 2
    for h in range(heads):
        for part in range(2):
            send[2 * h + part] = total[h, part * half : (part + 1) * half]


def scan_states(received, late, out):
    count = received.shape[0]
    half = C // 2
    state = jnp.zeros((half, C), f32)
    for k in range(count):
        out[k, :half] = state
        out[k, half:] = late[k]
        if k < count - 1:
            state = mul3(nt, halves(state), halves(received[k, :C])) + received[k, C:]


def scan_adjoints(maps, received, out):
    count = received.shape[0]
    half = C // 2
    state = jnp.zeros((half, C), f32)
    for k in reversed(range(count)):
        out[k] = state
        if k:
            state = mul3(nn, halves(state), halves(maps[k, :C])) + received[k, half:]


def query_grads(pair, heads, steps, query, key, value, grad, gain, incoming, inv, weight, trans, shift, cols, rows, norm_cols, scaled, fresh, starts, part, state, sums_so_far):
    step = pl.program_id(0)
    units = all_units(pair, heads)
    row, col = iotas()
    half = C // 2

    @pl.when(step == 0)
    def _():
        for h in range(heads):
            for side in range(2):
                state[h, side * half : (side + 1) * half] = incoming[2 * h + side, :half]

    for b in range(pair):
        for h in range(heads):
            starts[b, h] = state[h]
            state[h] = mul3(nt, halves(state[h]), halves(trans[b, h])) + shift[b, h]
    begin = [halves(starts[b, h]) for b, h in units]
    amounts = []
    for u, (b, h) in enumerate(units):
        amount = mul_left(nn, halves(inv[b, h]), tile(value, b, h)) - mul3(
            nt, halves(weight[b, h]), begin[u]
        )
        fresh[b, h] = amount
        amounts.append(halves(amount))
    cross = [mul_right(nt, tile(grad, b, h), amounts[u]) for u, (b, h) in enumerate(units)]
    sums = [jnp.zeros((C, 1), f32) for _ in range(pair)]
    for u, (b, h) in enumerate(units):
        here = cols[b * C : (b + 1) * C]
        g_col = here[:, h : h + 1]
        g_row = rows[b, h : h + 1]
        s_row = rows[b, heads + h : heads + h + 1]
        decayed = jnp.exp(jnp.where(row >= col, g_col - g_row, 0.0))
        mixed = jnp.where(row >= col, 2.0 * decayed * s_row * cross[u], 0.0)
        result = mul_left(nn, halves(mixed), tile(key, b, h)) + jnp.exp(g_col) * mul_right(
            nn, tile(grad, b, h), begin[u]
        )
        result = result * (gain[:, h * C : (h + 1) * C] * SCALE)
        scaled[b * C : (b + 1) * C, h * C : (h + 1) * C] = result
        sums[b] = sums[b] + jnp.sum(result * tile(query, b, h).astype(f32), axis=1, keepdims=True)
    for b in range(pair):
        full = sums[b] * norm_cols[b * C : (b + 1) * C]
        sums_so_far[pl.ds(step * pair + b, 1)] = full.T[:1]

    @pl.when(step == steps - 1)
    def _():
        part[...] = jnp.broadcast_to(sums_so_far[...][None], part.shape)


def finish_queries(pair, query, scaled, norm_cols, sums, others, out, corrections):
    step = pl.program_id(0)

    @pl.when(step == 0)
    def _():
        corrections[...] = jnp.sum(sums[...], axis=0) * (1.0 / D)

    lines = [corrections[pl.ds(step * pair + b, 1)] for b in range(pair)]
    columns = columns_of(jnp.concatenate(lines, axis=0))
    for b in range(pair):
        part = slice(b * C, (b + 1) * C)
        norm = norm_cols[part][:, :1]
        factor = norm * norm * columns[:, b : b + 1]
        out[part] = (norm * scaled[part] - query[part].astype(f32) * factor).astype(bf16)


def key_grads(pair, heads, query, key, grad, gain, outgoing, inv, trans, adjoint, inner, fresh, starts, cols, rows, norm_rows, out, state):
    step = pl.program_id(0)
    units = all_units(pair, heads)
    count = len(units)
    row, col = iotas()
    half = C // 2
    width = heads * C

    @pl.when(step == 0)
    def _():
        for h in range(heads):
            for side in range(2):
                state[h, side * half : (side + 1) * half] = outgoing[2 * h + side]

    ends = [None] * count
    for b in reversed(range(pair)):
        for h in range(heads):
            u = b * heads + h
            ends[u] = halves(state[h])
            state[h] = mul3(nn, ends[u], halves(trans[b, h])) + adjoint[b, h]
    g_row = [rows[b, h : h + 1] for b, h in units]
    s_row = [rows[b, heads + h : heads + h + 1] for b, h in units]
    keys = [tile(key, b, h) for b, h in units]
    amounts = [halves(fresh[b, h]) for b, h in units]
    turned = []
    for u, (b, h) in enumerate(units):
        end = jnp.exp(g_row[u][:, C - 1 :] - g_row[u]) * (2.0 * s_row[u])
        turned.append(halves(inner[b, h] + mul_left(nt, ends[u], keys[u]) * end))
    results = [mul3(nn, turned[u], halves(inv[b, h])).T for u, (b, h) in enumerate(units)]
    for u, (b, h) in enumerate(units):
        out[b * C : (b + 1) * C, 2 * width + h * C : 2 * width + (h + 1) * C] = results[u].astype(bf16)
    results = [halves(x) for x in results]
    against = [mul3(nt, results[u], amounts[u]) for u in range(count)]
    across = [mul_left(nt, amounts[u], tile(grad, b, h)) for u, (b, h) in enumerate(units)]
    for u, (b, h) in enumerate(units):
        here = cols[b * C : (b + 1) * C]
        g_col = here[:, h : h + 1]
        s_col = here[:, heads + h : heads + h + 1]
        n_row = norm_rows[b, :1]
        below = jnp.exp(jnp.where(row > col, g_col - g_row[u], 0.0))
        pulled = jnp.where(row > col, -2.0 * below * against[u], 0.0)
        both = (pulled + pulled.T) * s_row[u]
        above = jnp.exp(jnp.where(row <= col, g_row[u] - g_col, 0.0))
        mixed = jnp.where(row <= col, 2.0 * above * n_row * across[u], 0.0)
        total = mul_left(nn, halves(both), keys[u])
        total += mul_left(nn, halves(mixed), tile(query, b, h)) * (
            gain[:, h * C : (h + 1) * C] * SCALE
        )
        total -= jnp.exp(g_col) * mul3(nn, results[u], halves(starts[b, h]))
        end = 2.0 * jnp.exp(g_row[u][:, C - 1 :] - g_col)
        total += end * mul3(nn, amounts[u], ends[u])
        unit = keys[u].astype(f32) * s_col
        along = jnp.sum(unit * total, axis=1, keepdims=True)
        out[b * C : (b + 1) * C, width + h * C : width + (h + 1) * C] = (
            s_col * (total - unit * along)
        ).astype(bf16)


def per_device(query_raw, key_raw, value_raw, query_gain, log_decay, out_grad):
    rows, width = query_raw.shape
    heads = log_decay.shape[0]
    blocks = rows // C
    group = lax.axis_size(HEAD)
    chain = lax.axis_size(SEQ)
    gain = query_gain.reshape(1, width)
    shape = jax.ShapeDtypeStruct

    def specs(pair, reverse=False):
        steps = blocks // pair

        def at(i):
            return steps - 1 - i if reverse else i

        return (
            steps,
            pl.BlockSpec((pair * C, width), lambda i: (at(i), 0)),
            pl.BlockSpec((pair, heads, C, C), lambda i: (at(i), 0, 0, 0)),
            pl.BlockSpec((pair * C, C), lambda i: (at(i), 0)),
            pl.BlockSpec((pair, 8, C), lambda i: (at(i), 0, 0)),
        )

    def fixed(*block):
        return pl.BlockSpec(block, lambda i: (0,) * len(block))

    def exchange(value, axis):
        return lax.all_to_all(value, axis, 0, 0, tiled=True)

    matrices = shape((blocks, heads, C, C), f32)
    columns = shape((rows, C), f32)
    lines = shape((blocks, 8, C), f32)
    sums = shape((group, blocks, C), f32)
    carry = pltpu.VMEM((heads, C, C), f32)
    line_scratch = pltpu.VMEM((blocks, C), f32)
    half = C // 2

    squares = exchange(
        pl.pallas_call(square_sums, out_shape=sums, name="square_sums")(query_raw), HEAD
    )

    steps, tokens, matrix, column, line = specs(PAIRS[0])
    inv, weight, trans, shift, cols, row_info, send = pl.pallas_call(
        functools.partial(prep_keys, PAIRS[0], heads, steps),
        grid=(steps,),
        in_specs=[tokens, tokens, pl.BlockSpec((heads, PAIRS[0] * C), lambda i: (0, i))],
        out_specs=[matrix] * 4 + [column, line, fixed(2 * heads, C + half, C)],
        out_shape=[matrices] * 4 + [columns, lines, shape((2 * heads, C + half, C), f32)],
        scratch_shapes=[carry, carry],
        name="prep_keys",
    )(key_raw, value_raw, log_decay)
    maps = exchange(send, SEQ)

    steps, tokens, matrix, column, line = specs(PAIRS[1], reverse=True)
    inner, adjoint, norm_cols, norm_rows, late = pl.pallas_call(
        functools.partial(prep_queries, PAIRS[1], heads, steps),
        grid=(steps,),
        in_specs=[tokens] * 3
        + [fixed(1, width), fixed(group, blocks, C)]
        + [matrix, matrix, column, line],
        out_specs=[matrix, matrix, column, line, fixed(2 * heads, half, C)],
        out_shape=[matrices, matrices, columns, lines, shape((2 * heads, half, C), f32)],
        scratch_shapes=[carry, line_scratch],
        name="prep_queries",
    )(query_raw, key_raw, out_grad, gain, squares, weight, trans, cols, row_info)

    incoming = exchange(
        pl.pallas_call(scan_states, out_shape=shape((chain, C, C), f32), name="scan_states")(
            maps, late
        ),
        SEQ,
    )
    outgoing = exchange(
        pl.pallas_call(
            scan_adjoints, out_shape=shape((chain, half, C), f32), name="scan_adjoints"
        )(maps, incoming),
        SEQ,
    )

    steps, tokens, matrix, column, line = specs(PAIRS[2])
    scaled, fresh, starts, part = pl.pallas_call(
        functools.partial(query_grads, PAIRS[2], heads, steps),
        grid=(steps,),
        in_specs=[tokens] * 4
        + [fixed(1, width), fixed(2 * heads, C, C)]
        + [matrix] * 4
        + [column, line, column],
        out_specs=[tokens, matrix, matrix, fixed(group, blocks, C)],
        out_shape=[shape((rows, width), f32), matrices, matrices, sums],
        scratch_shapes=[carry, line_scratch],
        name="query_grads",
    )(
        query_raw, key_raw, value_raw, out_grad, gain, incoming,
        inv, weight, trans, shift, cols, row_info, norm_cols,
    )
    corrections = exchange(part, HEAD)

    steps, tokens, matrix, column, line = specs(PAIRS[4], reverse=True)
    key_value = pl.pallas_call(
        functools.partial(key_grads, PAIRS[4], heads),
        grid=(steps,),
        in_specs=[tokens] * 3
        + [fixed(1, width), fixed(2 * heads, half, C)]
        + [matrix] * 6
        + [column, line, line],
        out_specs=pl.BlockSpec((PAIRS[4] * C, 3 * width), lambda i: (steps - 1 - i, 0)),
        out_shape=shape((rows, 3 * width), bf16),
        scratch_shapes=[carry],
        name="key_grads",
    )(
        query_raw, key_raw, out_grad, gain, outgoing,
        inv, trans, adjoint, inner, fresh, starts, cols, row_info, norm_rows,
    )

    steps, tokens, matrix, column, line = specs(PAIRS[3])
    grads = pl.pallas_call(
        functools.partial(finish_queries, PAIRS[3]),
        grid=(steps,),
        in_specs=[tokens, tokens, column, fixed(group, blocks, C), pl.BlockSpec(memory_space=pl.ANY)],
        out_specs=tokens,
        out_shape=shape((rows, 3 * width), bf16),
        input_output_aliases={4: 0},
        scratch_shapes=[line_scratch],
        name="finish_queries",
    )(query_raw, scaled, norm_cols, corrections, key_value)

    pieces = exchange(grads.reshape(group, rows // group, 3 * width), HEAD)
    return tuple(
        pieces[:, :, at : at + width].transpose(1, 0, 2).reshape(rows // group, group * width)
        for at in range(0, 3 * width, width)
    )


def solution(mesh):
    split = Mesh(mesh.devices.reshape(4, 2, 4, 4), ("seq_0", "seq_1", "head_0", "head_1"))
    return jax.shard_map(
        per_device,
        mesh=split,
        in_specs=(P(SEQ, HEAD), P(SEQ, HEAD), P(SEQ, HEAD), P(HEAD), P(HEAD, SEQ), P(SEQ, HEAD)),
        out_specs=(P(SEQ_HEAD, None), P(SEQ_HEAD, None), P(SEQ_HEAD, None)),
        check_vma=False,
    )
```

```python
import functools

import jax
import jax.numpy as jnp
from jax import lax
from jax.experimental import pallas as pl
from jax.experimental.pallas import tpu as pltpu
from jax.sharding import Mesh
from jax.sharding import PartitionSpec as P


D = 8192
C = 128
PAIRS = (2, 2, 2, 4, 4)
HEAD = ("head_0", "head_1")
SEQ = ("seq_0", "seq_1")
SEQ_HEAD = ("seq_0", "seq_1", "head_0", "head_1")
EPS = 1e-06
SCALE = C ** (-0.5)

f32 = jnp.float32
bf16 = jnp.bfloat16


def halves(x):
    high = x.astype(bf16)
    return high, (x - high.astype(f32)).astype(bf16)


def nn(a, b):
    return lax.dot_general(a, b, (((1,), (0,)), ((), ())), preferred_element_type=f32)


def nt(a, b):
    return lax.dot_general(a, b, (((1,), (1,)), ((), ())), preferred_element_type=f32)


def mul3(form, a, b):
    return form(a[0], b[0]) + (form(a[0], b[1]) + form(a[1], b[0]))


def mul_left(form, a, b):
    return form(a[0], b) + form(a[1], b)


def mul_right(form, a, b):
    return form(a, b[0]) + form(a, b[1])


def iotas():
    return (
        lax.broadcasted_iota(jnp.int32, (C, C), 0),
        lax.broadcasted_iota(jnp.int32, (C, C), 1),
    )


def columns_of(rows):
    missing = C - rows.shape[0]
    return jnp.concatenate([rows, jnp.zeros((missing, C), f32)], axis=0).T


def tile(ref, b, h):
    return ref[b * C : (b + 1) * C, h * C : (h + 1) * C]


def square_sums(query, out):
    blocks = query.shape[0] // C
    ones = jnp.full((out.shape[0], query.shape[1]), 1.0, bf16)
    wide = query[...].astype(f32)
    sums = mul_right(nt, ones, halves(wide * wide))
    for b in range(blocks):
        out[:, b] = sums[:, b * C : (b + 1) * C]


def all_units(pair, heads):
    return [(b, h) for b in range(pair) for h in range(heads)]


def prep_keys(pair, heads, steps, place, key, value, decay, inv, weight, trans, shift, cols, rows, mine, other, whole, offset):
    step = pl.program_id(0)
    units = all_units(pair, heads)
    count = len(units)
    row, col = iotas()

    @pl.when(step == 0)
    def _():
        eye = jnp.where(row == col, 1.0, 0.0)
        for h in range(heads):
            whole[h] = eye
            offset[h] = jnp.zeros((C, C), f32)

    upto = jnp.where(row <= col, 1.0, 0.0)
    logs = jnp.concatenate([decay[:, b * C : (b + 1) * C] for b in range(pair)], axis=0)
    cumul_rows = jnp.dot(logs, upto, precision=lax.Precision.HIGHEST, preferred_element_type=f32)
    cumul_cols = columns_of(cumul_rows)

    raw = [tile(key, b, h) for b, h in units]
    scale_cols = []
    gathered = jnp.zeros((C, C), f32)
    for u in range(count):
        wide = raw[u].astype(f32)
        scale_cols.append(lax.rsqrt(jnp.sum(wide * wide, axis=1, keepdims=True) + EPS))
        gathered = jnp.where(col == u, scale_cols[u], gathered)
    scale_rows = gathered.T

    for b in range(pair):
        these = slice(b * heads, (b + 1) * heads)
        rows[b] = jnp.concatenate([cumul_rows[these], scale_rows[these]], axis=0)
        packed = jnp.zeros((C, C), f32)
        for h in range(heads):
            u = b * heads + h
            packed = jnp.where(col == h, cumul_cols[:, u : u + 1], packed)
            packed = jnp.where(col == heads + h, scale_cols[u], packed)
        cols[b * C : (b + 1) * C] = packed

    g_col = [cumul_cols[:, u : u + 1] for u in range(count)]
    g_row = [cumul_rows[u : u + 1] for u in range(count)]
    s_row = [scale_rows[u : u + 1] for u in range(count)]
    last = [g_row[u][:, C - 1 :] for u in range(count)]

    lower = []
    for u in range(count):
        gram = nt(raw[u], raw[u])
        decayed = jnp.exp(jnp.where(row > col, g_col[u] - g_row[u], 0.0))
        lower.append(
            jnp.where(row > col, 2.0 * decayed * (scale_cols[u] * s_row[u]) * gram, 0.0)
        )

    apart = row ^ col
    result = [
        jnp.where(row == col, 1.0, 0.0) - jnp.where(apart == 1, lower[u], 0.0) for u in range(count)
    ]
    size = 2
    while size < C:
        here = (apart >= size) & (apart < 2 * size)
        split = [halves(x) for x in result]
        below = [halves(jnp.where(here, lower[u], 0.0)) for u in range(count)]
        inner = [halves(mul3(nn, below[u], split[u])) for u in range(count)]
        result = [result[u] - mul3(nn, split[u], inner[u]) for u in range(count)]
        size *= 2

    split = [halves(x) for x in result]
    scaled, moved = [], []
    for u, (b, h) in enumerate(units):
        inv[b, h] = result[u]
        end = jnp.exp(last[u] - g_row[u])
        turned = tile(value, b, h).T
        amount = mul_right(nt, turned, split[u]) * (2.0 * end * s_row[u])
        moved.append(mul_left(nn, halves(amount), raw[u]))
        shift[b, h] = moved[u]
        start = jnp.exp(g_row[u]) * s_row[u]
        scaled.append(mul_left(nn, halves(result[u] * start), raw[u]))
        weight[b, h] = scaled[u]
    maps = []
    for u, (b, h) in enumerate(units):
        end = jnp.exp(last[u] - g_col[u]) * (2.0 * scale_cols[u])
        drop = mul_right(nn, raw[u].T, halves(scaled[u] * end))
        maps.append(jnp.where(row == col, jnp.exp(last[u]), 0.0) - drop)
        trans[b, h] = maps[u]

    for b in range(pair):
        for h in range(heads):
            u = b * heads + h
            step_map = halves(maps[u])
            whole[h] = mul3(nn, step_map, halves(whole[h]))
            offset[h] = mul3(nt, halves(offset[h]), step_map) + moved[u]

    @pl.when(step == steps - 1)
    def _():
        half = heads // 2
        first = place[1] * half
        for j in range(half):
            mine[j, 0] = whole[first + j]
            mine[j, 1] = offset[first + j]
            other[j, 0] = whole[half - first + j]
            other[j, 1] = offset[half - first + j]


def chip_maps(place, mine, other, out):
    first = place[1] == 0
    for j in range(mine.shape[0]):
        early = [jnp.where(first, mine[j, i], other[j, i]) for i in range(2)]
        late = [jnp.where(first, other[j, i], mine[j, i]) for i in range(2)]
        step_map = halves(late[0])
        out[j, 0] = mul3(nn, step_map, halves(early[0]))
        out[j, 1] = mul3(nt, halves(early[1]), step_map) + late[1]


def chip_states(place, mine, other, one, two, three, mine_back, other_back, stay, leave, back):
    first = place[1] == 0
    for j in range(mine.shape[0]):
        state = jnp.zeros((C, C), f32)
        for k, behind in ((3, three), (2, two), (1, one)):
            moved = mul3(nt, halves(state), halves(behind[j, 0])) + behind[j, 1]
            state = jnp.where(place[0] >= k, moved, state)
        early = [jnp.where(first, mine[j, i], other[j, i]) for i in range(2)]
        step_map = halves(early[0])
        after = mul3(nt, halves(state), step_map) + early[1]
        stay[j] = jnp.where(first, state, after)
        leave[j] = jnp.where(first, after, state)
        early_back = jnp.where(first, mine_back[j], other_back[j])
        late_back = jnp.where(first, other_back[j], mine_back[j])
        back[j] = mul3(nn, halves(late_back), step_map) + early_back


def chip_adjoints(last, place, mine, other, one, two, three, one_back, two_back, three_back, mine_back, other_back, stay, leave):
    first = place[1] == 0
    for j in range(mine.shape[0]):
        state = jnp.zeros((C, C), f32)
        for k, ahead, term in ((3, one, one_back), (2, two, two_back), (1, three, three_back)):
            moved = mul3(nn, halves(state), halves(ahead[j, 0])) + term[j]
            state = jnp.where(place[0] + k <= last, moved, state)
        late = jnp.where(first, other[j, 0], mine[j, 0])
        late_back = jnp.where(first, other_back[j], mine_back[j])
        before = mul3(nn, halves(state), halves(late)) + late_back
        stay[j] = jnp.where(first, before, state)
        leave[j] = jnp.where(first, state, before)


def prep_queries(pair, heads, steps, place, query, key, grad, gain, sums, weight, trans, cols, rows, inner, adjoint, norm_cols, norm_rows, mine, other, total, norms):
    step = pl.program_id(0)
    units = all_units(pair, heads)
    count = len(units)
    row, col = iotas()

    @pl.when(step == 0)
    def _():
        for h in range(heads):
            total[h] = jnp.zeros((C, C), f32)
        norms[...] = lax.rsqrt(jnp.sum(sums[...], axis=0) * (1.0 / D) + EPS)

    first = (steps - 1 - step) * pair
    n_rows = [norms[pl.ds(first + b, 1)] for b in range(pair)]
    n_cols = columns_of(jnp.concatenate(n_rows, axis=0))
    for b in range(pair):
        norm_rows[b] = jnp.broadcast_to(n_rows[b], (8, C))
        norm_cols[b * C : (b + 1) * C] = jnp.broadcast_to(n_cols[:, b : b + 1], (C, C))

    scaled_query, mixing = [], []
    for u, (b, h) in enumerate(units):
        here = cols[b * C : (b + 1) * C]
        g_col = here[:, h : h + 1]
        g_row = rows[b, h : h + 1]
        s_row = rows[b, heads + h : heads + h + 1]
        n_col = n_cols[:, b : b + 1]
        wide = tile(query, b, h).astype(f32) * (gain[:, h * C : (h + 1) * C] * SCALE)
        decayed = jnp.exp(jnp.where(row >= col, g_col - g_row, 0.0))
        scores = mul_left(nt, halves(wide), tile(key, b, h))
        mixing.append(
            halves(jnp.where(row >= col, 2.0 * decayed * (n_col * s_row) * scores, 0.0))
        )
        scaled_query.append(halves(wide * (jnp.exp(g_col) * n_col)))
    turned = [tile(grad, b, h).T for b, h in units]
    mixed = [mul_right(nn, turned[u], mixing[u]) for u in range(count)]
    terms = []
    for u, (b, h) in enumerate(units):
        inner[b, h] = mixed[u]
        terms.append(
            mul_right(nn, turned[u], scaled_query[u])
            - mul3(nn, halves(mixed[u]), halves(weight[b, h]))
        )
        adjoint[b, h] = terms[u]
    for b in reversed(range(pair)):
        for h in range(heads):
            u = b * heads + h
            total[h] = mul3(nn, halves(total[h]), halves(trans[b, h])) + terms[u]

    @pl.when(step == steps - 1)
    def _():
        half = heads // 2
        begin = place[1] * half
        for j in range(half):
            mine[j] = total[begin + j]
            other[j] = total[half - begin + j]


def query_grads(pair, heads, steps, place, query, key, value, grad, gain, mine, other, inv, weight, trans, shift, cols, rows, norm_cols, scaled, fresh, starts, part, state, sums_so_far):
    step = pl.program_id(0)
    units = all_units(pair, heads)
    row, col = iotas()

    @pl.when(step == 0)
    def _():
        half = heads // 2
        first = place[1] * half
        for j in range(half):
            state[first + j] = mine[j]
            state[half - first + j] = other[j]

    for b in range(pair):
        for h in range(heads):
            starts[b, h] = state[h]
            state[h] = mul3(nt, halves(state[h]), halves(trans[b, h])) + shift[b, h]
    begin = [halves(starts[b, h]) for b, h in units]
    amounts = []
    for u, (b, h) in enumerate(units):
        amount = mul_left(nn, halves(inv[b, h]), tile(value, b, h)) - mul3(
            nt, halves(weight[b, h]), begin[u]
        )
        fresh[b, h] = amount
        amounts.append(halves(amount))
    cross = [mul_right(nt, tile(grad, b, h), amounts[u]) for u, (b, h) in enumerate(units)]
    sums = [jnp.zeros((C, 1), f32) for _ in range(pair)]
    for u, (b, h) in enumerate(units):
        here = cols[b * C : (b + 1) * C]
        g_col = here[:, h : h + 1]
        g_row = rows[b, h : h + 1]
        s_row = rows[b, heads + h : heads + h + 1]
        decayed = jnp.exp(jnp.where(row >= col, g_col - g_row, 0.0))
        mixed = jnp.where(row >= col, 2.0 * decayed * s_row * cross[u], 0.0)
        result = mul_left(nn, halves(mixed), tile(key, b, h)) + jnp.exp(g_col) * mul_right(
            nn, tile(grad, b, h), begin[u]
        )
        result = result * (gain[:, h * C : (h + 1) * C] * SCALE)
        scaled[b * C : (b + 1) * C, h * C : (h + 1) * C] = result
        sums[b] = sums[b] + jnp.sum(result * tile(query, b, h).astype(f32), axis=1, keepdims=True)
    for b in range(pair):
        full = sums[b] * norm_cols[b * C : (b + 1) * C]
        sums_so_far[pl.ds(step * pair + b, 1)] = full.T[:1]

    @pl.when(step == steps - 1)
    def _():
        part[...] = jnp.broadcast_to(sums_so_far[...][None], part.shape)


def finish_queries(pair, query, scaled, norm_cols, sums, others, out, corrections):
    step = pl.program_id(0)

    @pl.when(step == 0)
    def _():
        corrections[...] = jnp.sum(sums[...], axis=0) * (1.0 / D)

    lines = [corrections[pl.ds(step * pair + b, 1)] for b in range(pair)]
    columns = columns_of(jnp.concatenate(lines, axis=0))
    for b in range(pair):
        part = slice(b * C, (b + 1) * C)
        norm = norm_cols[part][:, :1]
        factor = norm * norm * columns[:, b : b + 1]
        out[part] = (norm * scaled[part] - query[part].astype(f32) * factor).astype(bf16)


def key_grads(pair, heads, part, place, query, key, grad, gain, mine, other, inv, trans, adjoint, inner, fresh, starts, cols, rows, norm_rows, ready, out, state):
    step = pl.program_id(0)
    taken = heads // 2
    begin = part * taken
    units = all_units(pair, taken)
    count = len(units)
    row, col = iotas()
    width = taken * C

    @pl.when(step == 0)
    def _():
        own = place[1] == part
        for h in range(taken):
            state[h] = jnp.where(own, mine[h], other[h])

    ends = [None] * count
    for b in reversed(range(pair)):
        for h in range(taken):
            u = b * taken + h
            ends[u] = halves(state[h])
            state[h] = mul3(nn, ends[u], halves(trans[b, h])) + adjoint[b, h]
    g_row = [rows[b, begin + h : begin + h + 1] for b, h in units]
    s_row = [rows[b, heads + begin + h : heads + begin + h + 1] for b, h in units]
    keys = [tile(key, b, h) for b, h in units]
    amounts = [halves(fresh[b, h]) for b, h in units]
    turned = []
    for u, (b, h) in enumerate(units):
        end = jnp.exp(g_row[u][:, C - 1 :] - g_row[u]) * (2.0 * s_row[u])
        turned.append(halves(inner[b, h] + mul_left(nt, ends[u], keys[u]) * end))
    results = [mul3(nn, turned[u], halves(inv[b, h])).T for u, (b, h) in enumerate(units)]
    for u, (b, h) in enumerate(units):
        out[b * C : (b + 1) * C, width + h * C : width + (h + 1) * C] = results[u].astype(bf16)
    results = [halves(x) for x in results]
    against = [mul3(nt, results[u], amounts[u]) for u in range(count)]
    across = [mul_left(nt, amounts[u], tile(grad, b, h)) for u, (b, h) in enumerate(units)]
    for u, (b, h) in enumerate(units):
        here = cols[b * C : (b + 1) * C]
        g_col = here[:, begin + h : begin + h + 1]
        s_col = here[:, heads + begin + h : heads + begin + h + 1]
        n_row = norm_rows[b, :1]
        below = jnp.exp(jnp.where(row > col, g_col - g_row[u], 0.0))
        pulled = jnp.where(row > col, -2.0 * below * against[u], 0.0)
        both = (pulled + pulled.T) * s_row[u]
        above = jnp.exp(jnp.where(row <= col, g_row[u] - g_col, 0.0))
        mixed = jnp.where(row <= col, 2.0 * above * n_row * across[u], 0.0)
        total = mul_left(nn, halves(both), keys[u])
        total += mul_left(nn, halves(mixed), tile(query, b, h)) * (
            gain[:, h * C : (h + 1) * C] * SCALE
        )
        total -= jnp.exp(g_col) * mul3(nn, results[u], halves(starts[b, h]))
        end = 2.0 * jnp.exp(g_row[u][:, C - 1 :] - g_col)
        total += end * mul3(nn, amounts[u], ends[u])
        unit = keys[u].astype(f32) * s_col
        along = jnp.sum(unit * total, axis=1, keepdims=True)
        out[b * C : (b + 1) * C, h * C : (h + 1) * C] = (
            s_col * (total - unit * along)
        ).astype(bf16)


def per_device(query_raw, key_raw, value_raw, query_gain, log_decay, out_grad):
    rows, width = query_raw.shape
    heads = log_decay.shape[0]
    blocks = rows // C
    group = lax.axis_size(HEAD)
    gain = query_gain.reshape(1, width)
    shape = jax.ShapeDtypeStruct

    def specs(pair, reverse=False):
        steps = blocks // pair

        def at(i):
            return steps - 1 - i if reverse else i

        return (
            steps,
            pl.BlockSpec((pair * C, width), lambda i: (at(i), 0)),
            pl.BlockSpec((pair, heads, C, C), lambda i: (at(i), 0, 0, 0)),
            pl.BlockSpec((pair * C, C), lambda i: (at(i), 0)),
            pl.BlockSpec((pair, 8, C), lambda i: (at(i), 0, 0)),
        )

    def fixed(*block):
        return pl.BlockSpec(block, lambda i: (0,) * len(block))

    def exchange(value, axis):
        return lax.all_to_all(value, axis, 0, 0, tiled=True)

    matrices = shape((blocks, heads, C, C), f32)
    columns = shape((rows, C), f32)
    lines = shape((blocks, 8, C), f32)
    sums = shape((group, blocks, C), f32)
    carry = pltpu.VMEM((heads, C, C), f32)
    line_scratch = pltpu.VMEM((blocks, C), f32)

    cores = lax.axis_size("seq_1")
    chips = lax.axis_size("seq_0")
    assert (chips, cores) == (4, 2) and heads % 2 == 0
    some = heads // 2
    place = jnp.stack([lax.axis_index("seq_0"), lax.axis_index("seq_1")]).astype(jnp.int32)
    scalar = pl.BlockSpec(memory_space=pltpu.SMEM)
    pair_maps = shape((some, 2, C, C), f32)
    pair_states = shape((some, C, C), f32)

    def to_other_core(value):
        return lax.ppermute(value, "seq_1", [(0, 1), (1, 0)])

    def from_chips_behind(value):
        pieces = []
        for k in range(1, chips):
            pieces.append(
                lax.ppermute(value, "seq_0", [(i, (i + k) % chips) for i in range(chips)])
            )
        return pieces

    def small(kernel, out_shape, *operands):
        return pl.pallas_call(
            kernel,
            in_specs=[scalar] + [pl.BlockSpec(memory_space=pltpu.VMEM)] * (len(operands) - 1),
            out_shape=out_shape,
        )(*operands)

    squares = exchange(
        pl.pallas_call(square_sums, out_shape=sums, name="square_sums")(query_raw), HEAD
    )

    steps, tokens, matrix, column, line = specs(PAIRS[0])
    inv, weight, trans, shift, cols, row_info, mine, other = pl.pallas_call(
        functools.partial(prep_keys, PAIRS[0], heads, steps),
        grid=(steps,),
        in_specs=[scalar, tokens, tokens, pl.BlockSpec((heads, PAIRS[0] * C), lambda i: (0, i))],
        out_specs=[matrix] * 4 + [column, line] + [fixed(some, 2, C, C)] * 2,
        out_shape=[matrices] * 4 + [columns, lines, pair_maps, pair_maps],
        scratch_shapes=[carry, carry],
        name="prep_keys",
    )(place, key_raw, value_raw, log_decay)
    other = to_other_core(other)
    behind = from_chips_behind(small(chip_maps, pair_maps, place, mine, other))

    steps, tokens, matrix, column, line = specs(PAIRS[1], reverse=True)
    inner, adjoint, norm_cols, norm_rows, mine_back, other_back = pl.pallas_call(
        functools.partial(prep_queries, PAIRS[1], heads, steps),
        grid=(steps,),
        in_specs=[scalar]
        + [tokens] * 3
        + [fixed(1, width), fixed(group, blocks, C)]
        + [matrix, matrix, column, line],
        out_specs=[matrix, matrix, column, line] + [fixed(some, C, C)] * 2,
        out_shape=[matrices, matrices, columns, lines, pair_states, pair_states],
        scratch_shapes=[carry, line_scratch],
        name="prep_queries",
    )(place, query_raw, key_raw, out_grad, gain, squares, weight, trans, cols, row_info)
    other_back = to_other_core(other_back)
    stay, leave, back = small(
        chip_states, [pair_states] * 3,
        place, mine, other, *behind, mine_back, other_back,
    )
    arrived = to_other_core(leave)
    ahead = from_chips_behind(back)

    steps, tokens, matrix, column, line = specs(PAIRS[2])
    scaled, fresh, starts, part = pl.pallas_call(
        functools.partial(query_grads, PAIRS[2], heads, steps),
        grid=(steps,),
        in_specs=[scalar]
        + [tokens] * 4
        + [fixed(1, width), fixed(some, C, C), fixed(some, C, C)]
        + [matrix] * 4
        + [column, line, column],
        out_specs=[tokens, matrix, matrix, fixed(group, blocks, C)],
        out_shape=[shape((rows, width), f32), matrices, matrices, sums],
        scratch_shapes=[carry, line_scratch],
        name="query_grads",
    )(
        place, query_raw, key_raw, value_raw, out_grad, gain, stay, arrived,
        inv, weight, trans, shift, cols, row_info, norm_cols,
    )
    corrections = exchange(part, HEAD)

    stay, leave = small(
        functools.partial(chip_adjoints, chips - 1), [pair_states] * 2,
        place, mine, other, *behind, *ahead, mine_back, other_back,
    )
    arrived = to_other_core(leave)

    def key_half(index, out_shape, at, ready):
        pair = PAIRS[4]
        steps, _, _, column, line = specs(pair, reverse=True)
        tokens = pl.BlockSpec((pair * C, some * C), lambda i: (steps - 1 - i, index))
        matrix = pl.BlockSpec((pair, some, C, C), lambda i: (steps - 1 - i, index, 0, 0))
        return pl.pallas_call(
            functools.partial(key_grads, pair, heads, index),
            grid=(steps,),
            in_specs=[scalar]
            + [tokens] * 3
            + [pl.BlockSpec((1, some * C), lambda i: (0, index))]
            + [fixed(some, C, C)] * 2
            + [matrix] * 6
            + [column, line, line, pl.BlockSpec(memory_space=pl.ANY)],
            out_specs=pl.BlockSpec((pair * C, 2 * some * C), lambda i: (steps - 1 - i, at)),
            out_shape=shape((rows, out_shape), bf16),
            scratch_shapes=[pltpu.VMEM((some, C, C), f32)],
        )(
            place, query_raw, key_raw, out_grad, gain, stay, arrived,
            inv, trans, adjoint, inner, fresh, starts, cols, row_info, norm_rows, ready,
        )

    def owned(array):
        return exchange(array.reshape(group, rows // group, array.shape[1]), HEAD)

    first_half = key_half(0, width, 0, part)
    first = owned(first_half)
    second_half = key_half(1, 2 * width, 1, first_half)

    steps, tokens, matrix, column, line = specs(PAIRS[3])
    second = owned(
        pl.pallas_call(
            functools.partial(finish_queries, PAIRS[3]),
            grid=(steps,),
            in_specs=[
                tokens, tokens, column, fixed(group, blocks, C),
                pl.BlockSpec(memory_space=pl.ANY),
            ],
            out_specs=tokens,
            out_shape=shape((rows, 2 * width), bf16),
            input_output_aliases={4: 0},
            scratch_shapes=[line_scratch],
            name="finish_queries",
        )(query_raw, scaled, norm_cols, corrections, second_half),
    )

    def lay(*pieces):
        whole = pieces[0] if len(pieces) == 1 else jnp.concatenate(pieces, axis=2)
        return whole.transpose(1, 0, 2).reshape(rows // group, group * width)

    side = some * C
    return (
        lay(second[:, :, :width]),
        lay(first[:, :, :side], second[:, :, width : width + side]),
        lay(first[:, :, side:], second[:, :, width + side :]),
    )


def solution(mesh):
    split = Mesh(mesh.devices.reshape(4, 2, 4, 4), ("seq_0", "seq_1", "head_0", "head_1"))
    return jax.shard_map(
        per_device,
        mesh=split,
        in_specs=(P(SEQ, HEAD), P(SEQ, HEAD), P(SEQ, HEAD), P(HEAD), P(HEAD, SEQ), P(SEQ, HEAD)),
        out_specs=(P(SEQ_HEAD, None), P(SEQ_HEAD, None), P(SEQ_HEAD, None)),
        check_vma=False,
    )
```

```python
import functools

import jax
import jax.numpy as jnp
from jax import lax
from jax.experimental import pallas as pl
from jax.experimental.pallas import tpu as pltpu
from jax.sharding import Mesh
from jax.sharding import PartitionSpec as P


D = 8192
C = 128
PAIRS = (4, 2, 2, 4, 2)
HEAD = ("head_0", "head_1")
SEQ = ("seq_0", "seq_1")
SEQ_HEAD = ("seq_0", "seq_1", "head_0", "head_1")
EPS = 1e-06
SCALE = C ** (-0.5)

f32 = jnp.float32
bf16 = jnp.bfloat16


def halves(x):
    high = x.astype(bf16)
    return high, (x - high.astype(f32)).astype(bf16)


def nn(a, b):
    return lax.dot_general(a, b, (((1,), (0,)), ((), ())), preferred_element_type=f32)


def nt(a, b):
    return lax.dot_general(a, b, (((1,), (1,)), ((), ())), preferred_element_type=f32)


def mul3(form, a, b):
    left = jnp.concatenate(a, axis=1)
    blank = jnp.zeros_like(b[1])
    if form is nn:
        upper = jnp.concatenate([b[0], b[1]], axis=1)
        lower = jnp.concatenate([b[0], blank], axis=1)
    else:
        upper = jnp.concatenate([b[0], b[0]], axis=1)
        lower = jnp.concatenate([b[1], blank], axis=1)
    both = form(left, jnp.concatenate([upper, lower], axis=0))
    return both[:, :C] + both[:, C:]


def mul_left(form, a, b):
    return form(a[0], b) + form(a[1], b)


def mul_right(form, a, b):
    return form(a, b[0]) + form(a, b[1])


def iotas():
    return (
        lax.broadcasted_iota(jnp.int32, (C, C), 0),
        lax.broadcasted_iota(jnp.int32, (C, C), 1),
    )


def columns_of(rows):
    missing = C - rows.shape[0]
    return jnp.concatenate([rows, jnp.zeros((missing, C), f32)], axis=0).T


def tile(ref, b, h):
    return ref[b * C : (b + 1) * C, h * C : (h + 1) * C]


def square_sums(query, out):
    blocks = query.shape[0] // C
    ones = jnp.full((out.shape[0], query.shape[1]), 1.0, bf16)
    wide = query[...].astype(f32)
    sums = mul_right(nt, ones, halves(wide * wide))
    for b in range(blocks):
        out[:, b] = sums[:, b * C : (b + 1) * C]


def all_units(pair, heads):
    return [(b, h) for b in range(pair) for h in range(heads)]


def prep_keys(pair, heads, steps, place, key, value, decay, inv, weight, trans, shift, cols, rows, mine, other, whole, offset):
    step = pl.program_id(0)
    units = all_units(pair, heads)
    count = len(units)
    row, col = iotas()

    @pl.when(step == 0)
    def _():
        eye = jnp.where(row == col, 1.0, 0.0)
        for h in range(heads):
            whole[h] = eye
            offset[h] = jnp.zeros((C, C), f32)

    upto = jnp.where(row <= col, 1.0, 0.0)
    logs = jnp.concatenate([decay[:, b * C : (b + 1) * C] for b in range(pair)], axis=0)
    cumul_rows = jnp.dot(logs, upto, precision=lax.Precision.HIGHEST, preferred_element_type=f32)
    cumul_cols = columns_of(cumul_rows)

    raw = [tile(key, b, h) for b, h in units]
    scale_cols = []
    gathered = jnp.zeros((C, C), f32)
    for u in range(count):
        wide = raw[u].astype(f32)
        scale_cols.append(lax.rsqrt(jnp.sum(wide * wide, axis=1, keepdims=True) + EPS))
        gathered = jnp.where(col == u, scale_cols[u], gathered)
    scale_rows = gathered.T

    for b in range(pair):
        these = slice(b * heads, (b + 1) * heads)
        rows[b] = jnp.concatenate([cumul_rows[these], scale_rows[these]], axis=0)
        packed = jnp.zeros((C, C), f32)
        for h in range(heads):
            u = b * heads + h
            packed = jnp.where(col == h, cumul_cols[:, u : u + 1], packed)
            packed = jnp.where(col == heads + h, scale_cols[u], packed)
        cols[b * C : (b + 1) * C] = packed

    g_col = [cumul_cols[:, u : u + 1] for u in range(count)]
    g_row = [cumul_rows[u : u + 1] for u in range(count)]
    s_row = [scale_rows[u : u + 1] for u in range(count)]
    last = [g_row[u][:, C - 1 :] for u in range(count)]

    lower = []
    for u in range(count):
        gram = nt(raw[u], raw[u])
        decayed = jnp.exp(jnp.where(row > col, g_col[u] - g_row[u], 0.0))
        lower.append(
            jnp.where(row > col, 2.0 * decayed * (scale_cols[u] * s_row[u]) * gram, 0.0)
        )

    apart = row ^ col
    result = [
        jnp.where(row == col, 1.0, 0.0) - jnp.where(apart == 1, lower[u], 0.0) for u in range(count)
    ]
    size = 2
    while size < C:
        here = (apart >= size) & (apart < 2 * size)
        split = [halves(x) for x in result]
        below = [halves(jnp.where(here, lower[u], 0.0)) for u in range(count)]
        inner = [halves(mul3(nn, below[u], split[u])) for u in range(count)]
        result = [result[u] - mul3(nn, split[u], inner[u]) for u in range(count)]
        size *= 2

    split = [halves(x) for x in result]
    scaled, moved = [], []
    for u, (b, h) in enumerate(units):
        inv[b, h] = result[u]
        end = jnp.exp(last[u] - g_row[u])
        turned = tile(value, b, h).T
        amount = mul_right(nt, turned, split[u]) * (2.0 * end * s_row[u])
        moved.append(mul_left(nn, halves(amount), raw[u]))
        shift[b, h] = moved[u]
        start = jnp.exp(g_row[u]) * s_row[u]
        scaled.append(mul_left(nn, halves(result[u] * start), raw[u]))
        weight[b, h] = scaled[u]
    maps = []
    for u, (b, h) in enumerate(units):
        end = jnp.exp(last[u] - g_col[u]) * (2.0 * scale_cols[u])
        drop = mul_right(nn, raw[u].T, halves(scaled[u] * end))
        maps.append(jnp.where(row == col, jnp.exp(last[u]), 0.0) - drop)
        trans[b, h] = maps[u]

    for b in range(pair):
        for h in range(heads):
            u = b * heads + h
            step_map = halves(maps[u])
            whole[h] = mul3(nn, step_map, halves(whole[h]))
            offset[h] = mul3(nt, halves(offset[h]), step_map) + moved[u]

    @pl.when(step == steps - 1)
    def _():
        half = heads // 2
        first = place[1] * half
        for j in range(half):
            mine[j, 0] = whole[first + j]
            mine[j, 1] = offset[first + j]
            other[j, 0] = whole[half - first + j]
            other[j, 1] = offset[half - first + j]


def chip_maps(place, mine, other, out):
    first = place[1] == 0
    for j in range(mine.shape[0]):
        early = [jnp.where(first, mine[j, i], other[j, i]) for i in range(2)]
        late = [jnp.where(first, other[j, i], mine[j, i]) for i in range(2)]
        step_map = halves(late[0])
        out[j, 0] = mul3(nn, step_map, halves(early[0]))
        out[j, 1] = mul3(nt, halves(early[1]), step_map) + late[1]


def chip_states(place, mine, other, one, two, three, mine_back, other_back, stay, leave, back):
    first = place[1] == 0
    for j in range(mine.shape[0]):
        state = jnp.zeros((C, C), f32)
        for k, behind in ((3, three), (2, two), (1, one)):
            moved = mul3(nt, halves(state), halves(behind[j, 0])) + behind[j, 1]
            state = jnp.where(place[0] >= k, moved, state)
        early = [jnp.where(first, mine[j, i], other[j, i]) for i in range(2)]
        step_map = halves(early[0])
        after = mul3(nt, halves(state), step_map) + early[1]
        stay[j] = jnp.where(first, state, after)
        leave[j] = jnp.where(first, after, state)
        early_back = jnp.where(first, mine_back[j], other_back[j])
        late_back = jnp.where(first, other_back[j], mine_back[j])
        back[j] = mul3(nn, halves(late_back), step_map) + early_back


def chip_adjoints(last, place, mine, other, one, two, three, one_back, two_back, three_back, mine_back, other_back, stay, leave):
    first = place[1] == 0
    for j in range(mine.shape[0]):
        state = jnp.zeros((C, C), f32)
        for k, ahead, term in ((3, one, one_back), (2, two, two_back), (1, three, three_back)):
            moved = mul3(nn, halves(state), halves(ahead[j, 0])) + term[j]
            state = jnp.where(place[0] + k <= last, moved, state)
        late = jnp.where(first, other[j, 0], mine[j, 0])
        late_back = jnp.where(first, other_back[j], mine_back[j])
        before = mul3(nn, halves(state), halves(late)) + late_back
        stay[j] = jnp.where(first, before, state)
        leave[j] = jnp.where(first, state, before)


def prep_queries(pair, heads, steps, place, query, key, grad, gain, sums, weight, trans, cols, rows, inner, adjoint, norm_cols, norm_rows, mine, other, total, norms):
    step = pl.program_id(0)
    units = all_units(pair, heads)
    count = len(units)
    row, col = iotas()

    @pl.when(step == 0)
    def _():
        for h in range(heads):
            total[h] = jnp.zeros((C, C), f32)
        norms[...] = lax.rsqrt(jnp.sum(sums[...], axis=0) * (1.0 / D) + EPS)

    first = (steps - 1 - step) * pair
    n_rows = [norms[pl.ds(first + b, 1)] for b in range(pair)]
    n_cols = columns_of(jnp.concatenate(n_rows, axis=0))
    for b in range(pair):
        norm_rows[b] = jnp.broadcast_to(n_rows[b], (8, C))
        norm_cols[b * C : (b + 1) * C] = jnp.broadcast_to(n_cols[:, b : b + 1], (C, C))

    scaled_query, mixing = [], []
    for u, (b, h) in enumerate(units):
        here = cols[b * C : (b + 1) * C]
        g_col = here[:, h : h + 1]
        g_row = rows[b, h : h + 1]
        s_row = rows[b, heads + h : heads + h + 1]
        n_col = n_cols[:, b : b + 1]
        wide = tile(query, b, h).astype(f32) * (gain[:, h * C : (h + 1) * C] * SCALE)
        decayed = jnp.exp(jnp.where(row >= col, g_col - g_row, 0.0))
        scores = mul_left(nt, halves(wide), tile(key, b, h))
        mixing.append(
            halves(jnp.where(row >= col, 2.0 * decayed * (n_col * s_row) * scores, 0.0))
        )
        scaled_query.append(halves(wide * (jnp.exp(g_col) * n_col)))
    turned = [tile(grad, b, h).T for b, h in units]
    mixed = [mul_right(nn, turned[u], mixing[u]) for u in range(count)]
    terms = []
    for u, (b, h) in enumerate(units):
        inner[b, h] = mixed[u]
        terms.append(
            mul_right(nn, turned[u], scaled_query[u])
            - mul3(nn, halves(mixed[u]), halves(weight[b, h]))
        )
        adjoint[b, h] = terms[u]
    for b in reversed(range(pair)):
        for h in range(heads):
            u = b * heads + h
            total[h] = mul3(nn, halves(total[h]), halves(trans[b, h])) + terms[u]

    @pl.when(step == steps - 1)
    def _():
        half = heads // 2
        begin = place[1] * half
        for j in range(half):
            mine[j] = total[begin + j]
            other[j] = total[half - begin + j]


def query_grads(pair, heads, steps, place, query, key, value, grad, gain, mine, other, inv, weight, trans, shift, cols, rows, norm_cols, scaled, fresh, starts, part, state, sums_so_far):
    step = pl.program_id(0)
    units = all_units(pair, heads)
    row, col = iotas()

    @pl.when(step == 0)
    def _():
        half = heads // 2
        first = place[1] * half
        for j in range(half):
            state[first + j] = mine[j]
            state[half - first + j] = other[j]

    for b in range(pair):
        for h in range(heads):
            starts[b, h] = state[h]
            state[h] = mul3(nt, halves(state[h]), halves(trans[b, h])) + shift[b, h]
    begin = [halves(starts[b, h]) for b, h in units]
    amounts = []
    for u, (b, h) in enumerate(units):
        amount = mul_left(nn, halves(inv[b, h]), tile(value, b, h)) - mul3(
            nt, halves(weight[b, h]), begin[u]
        )
        fresh[b, h] = amount
        amounts.append(halves(amount))
    cross = [mul_right(nt, tile(grad, b, h), amounts[u]) for u, (b, h) in enumerate(units)]
    sums = [jnp.zeros((C, 1), f32) for _ in range(pair)]
    for u, (b, h) in enumerate(units):
        here = cols[b * C : (b + 1) * C]
        g_col = here[:, h : h + 1]
        g_row = rows[b, h : h + 1]
        s_row = rows[b, heads + h : heads + h + 1]
        decayed = jnp.exp(jnp.where(row >= col, g_col - g_row, 0.0))
        mixed = jnp.where(row >= col, 2.0 * decayed * s_row * cross[u], 0.0)
        result = mul_left(nn, halves(mixed), tile(key, b, h)) + jnp.exp(g_col) * mul_right(
            nn, tile(grad, b, h), begin[u]
        )
        result = result * (gain[:, h * C : (h + 1) * C] * SCALE)
        scaled[b * C : (b + 1) * C, h * C : (h + 1) * C] = result
        sums[b] = sums[b] + jnp.sum(result * tile(query, b, h).astype(f32), axis=1, keepdims=True)
    for b in range(pair):
        full = sums[b] * norm_cols[b * C : (b + 1) * C]
        sums_so_far[pl.ds(step * pair + b, 1)] = full.T[:1]

    @pl.when(step == steps - 1)
    def _():
        part[...] = jnp.broadcast_to(sums_so_far[...][None], part.shape)


def finish_queries(pair, query, scaled, norm_cols, sums, out, corrections):
    step = pl.program_id(0)

    @pl.when(step == 0)
    def _():
        corrections[...] = jnp.sum(sums[...], axis=0) * (1.0 / D)

    lines = [corrections[pl.ds(step * pair + b, 1)] for b in range(pair)]
    columns = columns_of(jnp.concatenate(lines, axis=0))
    for b in range(pair):
        part = slice(b * C, (b + 1) * C)
        norm = norm_cols[part][:, :1]
        factor = norm * norm * columns[:, b : b + 1]
        out[part] = (norm * scaled[part] - query[part].astype(f32) * factor).astype(bf16)


def key_grads(pair, heads, place, query, key, grad, gain, mine, other, inv, trans, adjoint, inner, fresh, starts, cols, rows, norm_rows, ready, out, state):
    step = pl.program_id(0)
    units = all_units(pair, heads)
    count = len(units)
    row, col = iotas()
    width = heads * C

    @pl.when(step == 0)
    def _():
        half = heads // 2
        first = place[1] * half
        for j in range(half):
            state[first + j] = mine[j]
            state[half - first + j] = other[j]

    ends = [None] * count
    for b in reversed(range(pair)):
        for h in range(heads):
            u = b * heads + h
            ends[u] = halves(state[h])
            state[h] = mul3(nn, ends[u], halves(trans[b, h])) + adjoint[b, h]
    g_row = [rows[b, h : h + 1] for b, h in units]
    s_row = [rows[b, heads + h : heads + h + 1] for b, h in units]
    keys = [tile(key, b, h) for b, h in units]
    amounts = [halves(fresh[b, h]) for b, h in units]
    turned = []
    for u, (b, h) in enumerate(units):
        end = jnp.exp(g_row[u][:, C - 1 :] - g_row[u]) * (2.0 * s_row[u])
        turned.append(halves(inner[b, h] + mul_left(nt, ends[u], keys[u]) * end))
    results = [mul3(nn, turned[u], halves(inv[b, h])).T for u, (b, h) in enumerate(units)]
    for u, (b, h) in enumerate(units):
        out[b * C : (b + 1) * C, width + h * C : width + (h + 1) * C] = results[u].astype(bf16)
    results = [halves(x) for x in results]
    against = [mul3(nt, results[u], amounts[u]) for u in range(count)]
    across = [mul_left(nt, amounts[u], tile(grad, b, h)) for u, (b, h) in enumerate(units)]
    for u, (b, h) in enumerate(units):
        here = cols[b * C : (b + 1) * C]
        g_col = here[:, h : h + 1]
        s_col = here[:, heads + h : heads + h + 1]
        n_row = norm_rows[b, :1]
        below = jnp.exp(jnp.where(row > col, g_col - g_row[u], 0.0))
        pulled = jnp.where(row > col, -2.0 * below * against[u], 0.0)
        both = (pulled + pulled.T) * s_row[u]
        above = jnp.exp(jnp.where(row <= col, g_row[u] - g_col, 0.0))
        mixed = jnp.where(row <= col, 2.0 * above * n_row * across[u], 0.0)
        total = mul_left(nn, halves(both), keys[u])
        total += mul_left(nn, halves(mixed), tile(query, b, h)) * (
            gain[:, h * C : (h + 1) * C] * SCALE
        )
        total -= jnp.exp(g_col) * mul3(nn, results[u], halves(starts[b, h]))
        end = 2.0 * jnp.exp(g_row[u][:, C - 1 :] - g_col)
        total += end * mul3(nn, amounts[u], ends[u])
        unit = keys[u].astype(f32) * s_col
        along = jnp.sum(unit * total, axis=1, keepdims=True)
        out[b * C : (b + 1) * C, h * C : (h + 1) * C] = (
            s_col * (total - unit * along)
        ).astype(bf16)


def per_device(query_raw, key_raw, value_raw, query_gain, log_decay, out_grad):
    rows, width = query_raw.shape
    heads = log_decay.shape[0]
    blocks = rows // C
    group = lax.axis_size(HEAD)
    gain = query_gain.reshape(1, width)
    shape = jax.ShapeDtypeStruct

    def specs(pair, reverse=False):
        steps = blocks // pair

        def at(i):
            return steps - 1 - i if reverse else i

        return (
            steps,
            pl.BlockSpec((pair * C, width), lambda i: (at(i), 0)),
            pl.BlockSpec((pair, heads, C, C), lambda i: (at(i), 0, 0, 0)),
            pl.BlockSpec((pair * C, C), lambda i: (at(i), 0)),
            pl.BlockSpec((pair, 8, C), lambda i: (at(i), 0, 0)),
        )

    def fixed(*block):
        return pl.BlockSpec(block, lambda i: (0,) * len(block))

    def exchange(value, axis):
        return lax.all_to_all(value, axis, 0, 0, tiled=True)

    matrices = shape((blocks, heads, C, C), f32)
    columns = shape((rows, C), f32)
    lines = shape((blocks, 8, C), f32)
    sums = shape((group, blocks, C), f32)
    carry = pltpu.VMEM((heads, C, C), f32)
    line_scratch = pltpu.VMEM((blocks, C), f32)

    cores = lax.axis_size("seq_1")
    chips = lax.axis_size("seq_0")
    assert (chips, cores) == (4, 2) and heads % 2 == 0
    some = heads // 2
    place = jnp.stack([lax.axis_index("seq_0"), lax.axis_index("seq_1")]).astype(jnp.int32)
    scalar = pl.BlockSpec(memory_space=pltpu.SMEM)
    pair_maps = shape((some, 2, C, C), f32)
    pair_states = shape((some, C, C), f32)

    def to_other_core(value):
        return lax.ppermute(value, "seq_1", [(0, 1), (1, 0)])

    def from_chips_behind(value):
        pieces = []
        for k in range(1, chips):
            pieces.append(
                lax.ppermute(value, "seq_0", [(i, (i + k) % chips) for i in range(chips)])
            )
        return pieces

    def small(kernel, out_shape, *operands):
        return pl.pallas_call(
            kernel,
            in_specs=[scalar] + [pl.BlockSpec(memory_space=pltpu.VMEM)] * (len(operands) - 1),
            out_shape=out_shape,
        )(*operands)

    squares = exchange(
        pl.pallas_call(square_sums, out_shape=sums, name="square_sums")(query_raw), HEAD
    )

    steps, tokens, matrix, column, line = specs(PAIRS[0])
    inv, weight, trans, shift, cols, row_info, mine, other = pl.pallas_call(
        functools.partial(prep_keys, PAIRS[0], heads, steps),
        grid=(steps,),
        in_specs=[scalar, tokens, tokens, pl.BlockSpec((heads, PAIRS[0] * C), lambda i: (0, i))],
        out_specs=[matrix] * 4 + [column, line] + [fixed(some, 2, C, C)] * 2,
        out_shape=[matrices] * 4 + [columns, lines, pair_maps, pair_maps],
        scratch_shapes=[carry, carry],
        name="prep_keys",
    )(place, key_raw, value_raw, log_decay)
    other = to_other_core(other)
    behind = from_chips_behind(small(chip_maps, pair_maps, place, mine, other))

    steps, tokens, matrix, column, line = specs(PAIRS[1], reverse=True)
    inner, adjoint, norm_cols, norm_rows, mine_back, other_back = pl.pallas_call(
        functools.partial(prep_queries, PAIRS[1], heads, steps),
        grid=(steps,),
        in_specs=[scalar]
        + [tokens] * 3
        + [fixed(1, width), fixed(group, blocks, C)]
        + [matrix, matrix, column, line],
        out_specs=[matrix, matrix, column, line] + [fixed(some, C, C)] * 2,
        out_shape=[matrices, matrices, columns, lines, pair_states, pair_states],
        scratch_shapes=[carry, line_scratch],
        name="prep_queries",
    )(place, query_raw, key_raw, out_grad, gain, squares, weight, trans, cols, row_info)
    other_back = to_other_core(other_back)
    stay, leave, back = small(
        chip_states, [pair_states] * 3,
        place, mine, other, *behind, mine_back, other_back,
    )
    arrived = to_other_core(leave)
    ahead = from_chips_behind(back)

    steps, tokens, matrix, column, line = specs(PAIRS[2])
    scaled, fresh, starts, part = pl.pallas_call(
        functools.partial(query_grads, PAIRS[2], heads, steps),
        grid=(steps,),
        in_specs=[scalar]
        + [tokens] * 4
        + [fixed(1, width), fixed(some, C, C), fixed(some, C, C)]
        + [matrix] * 4
        + [column, line, column],
        out_specs=[tokens, matrix, matrix, fixed(group, blocks, C)],
        out_shape=[shape((rows, width), f32), matrices, matrices, sums],
        scratch_shapes=[carry, line_scratch],
        name="query_grads",
    )(
        place, query_raw, key_raw, value_raw, out_grad, gain, stay, arrived,
        inv, weight, trans, shift, cols, row_info, norm_cols,
    )
    corrections = exchange(part, HEAD)

    stay, leave = small(
        functools.partial(chip_adjoints, chips - 1), [pair_states] * 2,
        place, mine, other, *behind, *ahead, mine_back, other_back,
    )
    arrived = to_other_core(leave)

    def owned(array):
        return exchange(array.reshape(group, rows // group, array.shape[1]), HEAD)

    steps, tokens, matrix, column, line = specs(PAIRS[3])
    query_raw_grad = pl.pallas_call(
        functools.partial(finish_queries, PAIRS[3]),
        grid=(steps,),
        in_specs=[tokens, tokens, column, fixed(group, blocks, C)],
        out_specs=tokens,
        out_shape=shape((rows, width), bf16),
        scratch_shapes=[line_scratch],
        name="finish_queries",
    )(query_raw, scaled, norm_cols, corrections)
    first = owned(query_raw_grad)

    steps, tokens, matrix, column, line = specs(PAIRS[4], reverse=True)
    key_value = pl.pallas_call(
        functools.partial(key_grads, PAIRS[4], heads),
        grid=(steps,),
        in_specs=[scalar]
        + [tokens] * 3
        + [fixed(1, width), fixed(some, C, C), fixed(some, C, C)]
        + [matrix] * 6
        + [column, line, line, pl.BlockSpec(memory_space=pl.ANY)],
        out_specs=pl.BlockSpec((PAIRS[4] * C, 2 * width), lambda i: (steps - 1 - i, 0)),
        out_shape=shape((rows, 2 * width), bf16),
        scratch_shapes=[carry],
        name="key_grads",
    )(
        place, query_raw, key_raw, out_grad, gain, stay, arrived,
        inv, trans, adjoint, inner, fresh, starts, cols, row_info, norm_rows, query_raw_grad,
    )
    second = owned(key_value)

    def lay(pieces):
        return pieces.transpose(1, 0, 2).reshape(rows // group, group * width)

    return lay(first), lay(second[:, :, :width]), lay(second[:, :, width:])


def solution(mesh):
    split = Mesh(mesh.devices.reshape(4, 2, 4, 4), ("seq_0", "seq_1", "head_0", "head_1"))
    return jax.shard_map(
        per_device,
        mesh=split,
        in_specs=(P(SEQ, HEAD), P(SEQ, HEAD), P(SEQ, HEAD), P(HEAD), P(HEAD, SEQ), P(SEQ, HEAD)),
        out_specs=(P(SEQ_HEAD, None), P(SEQ_HEAD, None), P(SEQ_HEAD, None)),
        check_vma=False,
    )
```

```python
import functools

import jax
import jax.numpy as jnp
from jax import lax
from jax.experimental import pallas as pl
from jax.experimental.pallas import tpu as pltpu
from jax.sharding import Mesh
from jax.sharding import PartitionSpec as P


D = 8192
C = 128
PAIRS = (4, 2, 2, 4, 2)
HEAD = ("head_0", "head_1")
SEQ = ("seq_0", "seq_1")
SEQ_HEAD = ("seq_0", "seq_1", "head_0", "head_1")
EPS = 1e-06
BASE = 16
SCALE = C ** (-0.5)

f32 = jnp.float32
bf16 = jnp.bfloat16


def halves(x):
    high = x.astype(bf16)
    return high, (x - high.astype(f32)).astype(bf16)


def nn(a, b):
    return lax.dot_general(a, b, (((1,), (0,)), ((), ())), preferred_element_type=f32)


def nt(a, b):
    return lax.dot_general(a, b, (((1,), (1,)), ((), ())), preferred_element_type=f32)


def mul3(form, a, b):
    left = jnp.concatenate(a, axis=1)
    blank = jnp.zeros_like(b[1])
    if form is nn:
        upper = jnp.concatenate([b[0], b[1]], axis=1)
        lower = jnp.concatenate([b[0], blank], axis=1)
    else:
        upper = jnp.concatenate([b[0], b[0]], axis=1)
        lower = jnp.concatenate([b[1], blank], axis=1)
    both = form(left, jnp.concatenate([upper, lower], axis=0))
    return both[:, :C] + both[:, C:]


def mul_left(form, a, b):
    return form(a[0], b) + form(a[1], b)


def mul_right(form, a, b):
    return form(a, b[0]) + form(a, b[1])


def iotas():
    return (
        lax.broadcasted_iota(jnp.int32, (C, C), 0),
        lax.broadcasted_iota(jnp.int32, (C, C), 1),
    )


def columns_of(rows):
    missing = C - rows.shape[0]
    return jnp.concatenate([rows, jnp.zeros((missing, C), f32)], axis=0).T


def tile(ref, b, h):
    return ref[b * C : (b + 1) * C, h * C : (h + 1) * C]


def square_sums(heads, query, out, lines):
    step = pl.program_id(0)
    blocks = query.shape[0] // C
    for b in range(blocks):
        total = jnp.zeros((C, C), f32)
        for h in range(heads):
            wide = tile(query, b, h).astype(f32)
            total += wide * wide
        lines[pl.ds(step * blocks + b, 1)] = jnp.sum(total.T, axis=0, keepdims=True)

    @pl.when(step == pl.num_programs(0) - 1)
    def _():
        out[...] = jnp.broadcast_to(lines[...][None], out.shape)


def placed(kernel, *settings):
    def run(*refs):
        kernel(*settings, (lax.axis_index("seq_0"), lax.axis_index("seq_1")), *refs)

    return run


def all_units(pair, heads):
    return [(b, h) for b in range(pair) for h in range(heads)]


def block_inverses(lower):
    row, col = iotas()
    inside = (row // BASE) == (col // BASE)
    packed = jnp.sum(jnp.where(inside, lower, 0.0).reshape(C // BASE, BASE, C), axis=0)
    place_row = lax.broadcasted_iota(jnp.int32, (BASE, C), 0)
    place_col = lax.broadcasted_iota(jnp.int32, (BASE, C), 1)
    result = jnp.where(place_row == place_col % BASE, 1.0, 0.0)
    for j in range(BASE - 1):
        entry = (place_col // BASE) * BASE + j
        factor = jnp.take_along_axis(packed, entry, axis=1, mode="promise_in_bounds")
        result = result - factor * result[j : j + 1]
    return jnp.where(inside, jnp.concatenate([result] * (C // BASE), axis=0), 0.0)


def prep_keys(pair, heads, steps, place, key, value, decay, inv, weight, trans, shift, cols, rows, mine, other, whole, offset):
    step = pl.program_id(0)
    units = all_units(pair, heads)
    count = len(units)
    row, col = iotas()

    @pl.when(step == 0)
    def _():
        eye = jnp.where(row == col, 1.0, 0.0)
        for h in range(heads):
            whole[h] = eye
            offset[h] = jnp.zeros((C, C), f32)

    upto = jnp.where(row <= col, 1.0, 0.0)
    logs = jnp.concatenate([decay[:, b * C : (b + 1) * C] for b in range(pair)], axis=0)
    cumul_rows = jnp.dot(logs, upto, precision=lax.Precision.HIGHEST, preferred_element_type=f32)
    cumul_cols = columns_of(cumul_rows)

    raw = [tile(key, b, h) for b, h in units]
    scale_cols = []
    gathered = jnp.zeros((C, C), f32)
    for u in range(count):
        wide = raw[u].astype(f32)
        scale_cols.append(lax.rsqrt(jnp.sum(wide * wide, axis=1, keepdims=True) + EPS))
        gathered = jnp.where(col == u, scale_cols[u], gathered)
    scale_rows = gathered.T

    for b in range(pair):
        these = slice(b * heads, (b + 1) * heads)
        rows[b] = jnp.concatenate([cumul_rows[these], scale_rows[these]], axis=0)
        packed = jnp.zeros((C, C), f32)
        for h in range(heads):
            u = b * heads + h
            packed = jnp.where(col == h, cumul_cols[:, u : u + 1], packed)
            packed = jnp.where(col == heads + h, scale_cols[u], packed)
        cols[b * C : (b + 1) * C] = packed

    g_col = [cumul_cols[:, u : u + 1] for u in range(count)]
    g_row = [cumul_rows[u : u + 1] for u in range(count)]
    s_row = [scale_rows[u : u + 1] for u in range(count)]
    last = [g_row[u][:, C - 1 :] for u in range(count)]

    lower = []
    for u in range(count):
        gram = nt(raw[u], raw[u])
        decayed = jnp.exp(jnp.where(row > col, g_col[u] - g_row[u], 0.0))
        lower.append(
            jnp.where(row > col, 2.0 * decayed * (scale_cols[u] * s_row[u]) * gram, 0.0)
        )

    apart = row ^ col
    result = [block_inverses(lower[u]) for u in range(count)]
    size = BASE
    while size < C:
        here = (apart >= size) & (apart < 2 * size)
        split = [halves(x) for x in result]
        below = [halves(jnp.where(here, lower[u], 0.0)) for u in range(count)]
        inner = [halves(mul3(nn, below[u], split[u])) for u in range(count)]
        result = [result[u] - mul3(nn, split[u], inner[u]) for u in range(count)]
        size *= 2

    split = [halves(x) for x in result]
    scaled, moved = [], []
    for u, (b, h) in enumerate(units):
        inv[b, h] = result[u]
        end = jnp.exp(last[u] - g_row[u])
        turned = tile(value, b, h).T
        amount = mul_right(nt, turned, split[u]) * (2.0 * end * s_row[u])
        moved.append(mul_left(nn, halves(amount), raw[u]))
        shift[b, h] = moved[u]
        start = jnp.exp(g_row[u]) * s_row[u]
        scaled.append(mul_left(nn, halves(result[u] * start), raw[u]))
        weight[b, h] = scaled[u]
    maps = []
    for u, (b, h) in enumerate(units):
        end = jnp.exp(last[u] - g_col[u]) * (2.0 * scale_cols[u])
        drop = mul_right(nn, raw[u].T, halves(scaled[u] * end))
        maps.append(jnp.where(row == col, jnp.exp(last[u]), 0.0) - drop)
        trans[b, h] = maps[u]

    for b in range(pair):
        for h in range(heads):
            u = b * heads + h
            step_map = halves(maps[u])
            whole[h] = mul3(nn, step_map, halves(whole[h]))
            offset[h] = mul3(nt, halves(offset[h]), step_map) + moved[u]

    @pl.when(step == steps - 1)
    def _():
        half = heads // 2
        first = place[1] * half
        for j in range(half):
            mine[j, 0] = whole[first + j]
            mine[j, 1] = offset[first + j]
            other[j, 0] = whole[half - first + j]
            other[j, 1] = offset[half - first + j]


def chip_maps(place, mine, other, out):
    first = place[1] == 0
    for j in range(mine.shape[0]):
        early = [jnp.where(first, mine[j, i], other[j, i]) for i in range(2)]
        late = [jnp.where(first, other[j, i], mine[j, i]) for i in range(2)]
        step_map = halves(late[0])
        out[j, 0] = mul3(nn, step_map, halves(early[0]))
        out[j, 1] = mul3(nt, halves(early[1]), step_map) + late[1]


def chip_states(place, mine, other, one, two, three, mine_back, other_back, stay, leave, back):
    first = place[1] == 0
    for j in range(mine.shape[0]):
        state = jnp.zeros((C, C), f32)
        for k, behind in ((3, three), (2, two), (1, one)):
            moved = mul3(nt, halves(state), halves(behind[j, 0])) + behind[j, 1]
            state = jnp.where(place[0] >= k, moved, state)
        early = [jnp.where(first, mine[j, i], other[j, i]) for i in range(2)]
        step_map = halves(early[0])
        after = mul3(nt, halves(state), step_map) + early[1]
        stay[j] = jnp.where(first, state, after)
        leave[j] = jnp.where(first, after, state)
        early_back = jnp.where(first, mine_back[j], other_back[j])
        late_back = jnp.where(first, other_back[j], mine_back[j])
        back[j] = mul3(nn, halves(late_back), step_map) + early_back


def chip_adjoints(last, place, mine, other, one, two, three, one_back, two_back, three_back, mine_back, other_back, stay, leave):
    first = place[1] == 0
    for j in range(mine.shape[0]):
        state = jnp.zeros((C, C), f32)
        for k, ahead, term in ((3, one, one_back), (2, two, two_back), (1, three, three_back)):
            moved = mul3(nn, halves(state), halves(ahead[j, 0])) + term[j]
            state = jnp.where(place[0] + k <= last, moved, state)
        late = jnp.where(first, other[j, 0], mine[j, 0])
        late_back = jnp.where(first, other_back[j], mine_back[j])
        before = mul3(nn, halves(state), halves(late)) + late_back
        stay[j] = jnp.where(first, before, state)
        leave[j] = jnp.where(first, state, before)


def prep_queries(pair, heads, steps, place, query, key, grad, gain, sums, weight, trans, cols, rows, inner, adjoint, norm_cols, norm_rows, mine, other, total, norms):
    step = pl.program_id(0)
    units = all_units(pair, heads)
    count = len(units)
    row, col = iotas()

    @pl.when(step == 0)
    def _():
        for h in range(heads):
            total[h] = jnp.zeros((C, C), f32)
        norms[...] = lax.rsqrt(jnp.sum(sums[...], axis=0) * (1.0 / D) + EPS)

    first = (steps - 1 - step) * pair
    n_rows = [norms[pl.ds(first + b, 1)] for b in range(pair)]
    n_cols = columns_of(jnp.concatenate(n_rows, axis=0))
    for b in range(pair):
        norm_rows[b] = jnp.broadcast_to(n_rows[b], (8, C))
        norm_cols[b * C : (b + 1) * C] = jnp.broadcast_to(n_cols[:, b : b + 1], (C, C))

    scaled_query, mixing = [], []
    for u, (b, h) in enumerate(units):
        here = cols[b * C : (b + 1) * C]
        g_col = here[:, h : h + 1]
        g_row = rows[b, h : h + 1]
        s_row = rows[b, heads + h : heads + h + 1]
        n_col = n_cols[:, b : b + 1]
        wide = tile(query, b, h).astype(f32) * (gain[:, h * C : (h + 1) * C] * SCALE)
        decayed = jnp.exp(jnp.where(row >= col, g_col - g_row, 0.0))
        scores = mul_left(nt, halves(wide), tile(key, b, h))
        mixing.append(
            halves(jnp.where(row >= col, 2.0 * decayed * (n_col * s_row) * scores, 0.0))
        )
        scaled_query.append(halves(wide * (jnp.exp(g_col) * n_col)))
    turned = [tile(grad, b, h).T for b, h in units]
    mixed = [mul_right(nn, turned[u], mixing[u]) for u in range(count)]
    terms = []
    for u, (b, h) in enumerate(units):
        inner[b, h] = mixed[u]
        terms.append(
            mul_right(nn, turned[u], scaled_query[u])
            - mul3(nn, halves(mixed[u]), halves(weight[b, h]))
        )
        adjoint[b, h] = terms[u]
    for b in reversed(range(pair)):
        for h in range(heads):
            u = b * heads + h
            total[h] = mul3(nn, halves(total[h]), halves(trans[b, h])) + terms[u]

    @pl.when(step == steps - 1)
    def _():
        half = heads // 2
        begin = place[1] * half
        for j in range(half):
            mine[j] = total[begin + j]
            other[j] = total[half - begin + j]


def query_grads(pair, heads, steps, place, query, key, value, grad, gain, mine, other, inv, weight, trans, shift, cols, rows, norm_cols, scaled, fresh, starts, part, state, sums_so_far):
    step = pl.program_id(0)
    units = all_units(pair, heads)
    row, col = iotas()

    @pl.when(step == 0)
    def _():
        half = heads // 2
        first = place[1] * half
        for j in range(half):
            state[first + j] = mine[j]
            state[half - first + j] = other[j]

    for b in range(pair):
        for h in range(heads):
            starts[b, h] = state[h]
            state[h] = mul3(nt, halves(state[h]), halves(trans[b, h])) + shift[b, h]
    begin = [halves(starts[b, h]) for b, h in units]
    amounts = []
    for u, (b, h) in enumerate(units):
        amount = mul_left(nn, halves(inv[b, h]), tile(value, b, h)) - mul3(
            nt, halves(weight[b, h]), begin[u]
        )
        fresh[b, h] = amount
        amounts.append(halves(amount))
    cross = [mul_right(nt, tile(grad, b, h), amounts[u]) for u, (b, h) in enumerate(units)]
    sums = [jnp.zeros((C, 1), f32) for _ in range(pair)]
    for u, (b, h) in enumerate(units):
        here = cols[b * C : (b + 1) * C]
        g_col = here[:, h : h + 1]
        g_row = rows[b, h : h + 1]
        s_row = rows[b, heads + h : heads + h + 1]
        decayed = jnp.exp(jnp.where(row >= col, g_col - g_row, 0.0))
        mixed = jnp.where(row >= col, 2.0 * decayed * s_row * cross[u], 0.0)
        result = mul_left(nn, halves(mixed), tile(key, b, h)) + jnp.exp(g_col) * mul_right(
            nn, tile(grad, b, h), begin[u]
        )
        result = result * (gain[:, h * C : (h + 1) * C] * SCALE)
        scaled[b * C : (b + 1) * C, h * C : (h + 1) * C] = result
        sums[b] = sums[b] + jnp.sum(result * tile(query, b, h).astype(f32), axis=1, keepdims=True)
    for b in range(pair):
        full = sums[b] * norm_cols[b * C : (b + 1) * C]
        sums_so_far[pl.ds(step * pair + b, 1)] = full.T[:1]

    @pl.when(step == steps - 1)
    def _():
        part[...] = jnp.broadcast_to(sums_so_far[...][None], part.shape)


def finish_queries(pair, heads, query, scaled, norm_cols, sums, out, corrections):
    step = pl.program_id(0)

    @pl.when(step == 0)
    def _():
        corrections[...] = jnp.sum(sums[...], axis=0) * (1.0 / D)

    lines = [corrections[pl.ds(step * pair + b, 1)] for b in range(pair)]
    columns = columns_of(jnp.concatenate(lines, axis=0))
    for b in range(pair):
        part = slice(b * C, (b + 1) * C)
        norm = norm_cols[part]
        factor = norm * norm * columns[:, b : b + 1]
        for h in range(heads):
            side = slice(h * C, (h + 1) * C)
            out[part, side] = (
                norm * scaled[part, side] - query[part, side].astype(f32) * factor
            ).astype(bf16)


def key_grads(pair, heads, place, query, key, grad, gain, mine, other, inv, trans, adjoint, inner, fresh, starts, cols, rows, norm_rows, ready, out, state):
    step = pl.program_id(0)
    units = all_units(pair, heads)
    count = len(units)
    row, col = iotas()
    width = heads * C

    @pl.when(step == 0)
    def _():
        half = heads // 2
        first = place[1] * half
        for j in range(half):
            state[first + j] = mine[j]
            state[half - first + j] = other[j]

    ends = [None] * count
    for b in reversed(range(pair)):
        for h in range(heads):
            u = b * heads + h
            ends[u] = halves(state[h])
            state[h] = mul3(nn, ends[u], halves(trans[b, h])) + adjoint[b, h]
    g_row = [rows[b, h : h + 1] for b, h in units]
    s_row = [rows[b, heads + h : heads + h + 1] for b, h in units]
    keys = [tile(key, b, h) for b, h in units]
    amounts = [halves(fresh[b, h]) for b, h in units]
    turned = []
    for u, (b, h) in enumerate(units):
        end = jnp.exp(g_row[u][:, C - 1 :] - g_row[u]) * (2.0 * s_row[u])
        turned.append(halves(inner[b, h] + mul_left(nt, ends[u], keys[u]) * end))
    results = [mul3(nn, turned[u], halves(inv[b, h])).T for u, (b, h) in enumerate(units)]
    for u, (b, h) in enumerate(units):
        out[b * C : (b + 1) * C, width + h * C : width + (h + 1) * C] = results[u].astype(bf16)
    results = [halves(x) for x in results]
    against = [mul3(nt, results[u], amounts[u]) for u in range(count)]
    across = [mul_left(nt, amounts[u], tile(grad, b, h)) for u, (b, h) in enumerate(units)]
    for u, (b, h) in enumerate(units):
        here = cols[b * C : (b + 1) * C]
        g_col = here[:, h : h + 1]
        s_col = here[:, heads + h : heads + h + 1]
        n_row = norm_rows[b, :1]
        below = jnp.exp(jnp.where(row > col, g_col - g_row[u], 0.0))
        pulled = jnp.where(row > col, -2.0 * below * against[u], 0.0)
        both = (pulled + pulled.T) * s_row[u]
        above = jnp.exp(jnp.where(row <= col, g_row[u] - g_col, 0.0))
        mixed = jnp.where(row <= col, 2.0 * above * n_row * across[u], 0.0)
        total = mul_left(nn, halves(both), keys[u])
        total += mul_left(nn, halves(mixed), tile(query, b, h)) * (
            gain[:, h * C : (h + 1) * C] * SCALE
        )
        total -= jnp.exp(g_col) * mul3(nn, results[u], halves(starts[b, h]))
        end = 2.0 * jnp.exp(g_row[u][:, C - 1 :] - g_col)
        total += end * mul3(nn, amounts[u], ends[u])
        unit = keys[u].astype(f32) * s_col
        along = jnp.sum(unit * total, axis=1, keepdims=True)
        out[b * C : (b + 1) * C, h * C : (h + 1) * C] = (
            s_col * (total - unit * along)
        ).astype(bf16)


def per_device(query_raw, key_raw, value_raw, query_gain, log_decay, out_grad):
    rows, width = query_raw.shape
    heads = log_decay.shape[0]
    blocks = rows // C
    group = lax.axis_size(HEAD)
    gain = query_gain.reshape(1, width)
    shape = jax.ShapeDtypeStruct

    def specs(pair, reverse=False):
        steps = blocks // pair

        def at(i):
            return steps - 1 - i if reverse else i

        return (
            steps,
            pl.BlockSpec((pair * C, width), lambda i: (at(i), 0)),
            pl.BlockSpec((pair, heads, C, C), lambda i: (at(i), 0, 0, 0)),
            pl.BlockSpec((pair * C, C), lambda i: (at(i), 0)),
            pl.BlockSpec((pair, 8, C), lambda i: (at(i), 0, 0)),
        )

    def fixed(*block):
        return pl.BlockSpec(block, lambda i: (0,) * len(block))

    def exchange(value, axis):
        return lax.all_to_all(value, axis, 0, 0, tiled=True)

    matrices = shape((blocks, heads, C, C), f32)
    columns = shape((rows, C), f32)
    lines = shape((blocks, 8, C), f32)
    sums = shape((group, blocks, C), f32)
    carry = pltpu.VMEM((heads, C, C), f32)
    line_scratch = pltpu.VMEM((blocks, C), f32)

    cores = lax.axis_size("seq_1")
    chips = lax.axis_size("seq_0")
    assert (chips, cores) == (4, 2) and heads % 2 == 0
    some = heads // 2
    pair_maps = shape((some, 2, C, C), f32)
    pair_states = shape((some, C, C), f32)

    def to_other_core(value):
        return lax.ppermute(value, "seq_1", [(0, 1), (1, 0)])

    def from_chips_behind(value):
        pieces = []
        for k in range(1, chips):
            pieces.append(
                lax.ppermute(value, "seq_0", [(i, (i + k) % chips) for i in range(chips)])
            )
        return pieces

    def small(kernel, out_shape, *operands):
        return pl.pallas_call(
            kernel,
            in_specs=[pl.BlockSpec(memory_space=pltpu.VMEM)] * len(operands),
            out_shape=out_shape,
        )(*operands)

    squares = exchange(
        pl.pallas_call(
            functools.partial(square_sums, heads),
            grid=(2,),
            in_specs=[pl.BlockSpec((rows // 2, width), lambda i: (i, 0))],
            out_specs=fixed(group, blocks, C),
            out_shape=sums,
            scratch_shapes=[line_scratch],
            name="square_sums",
        )(query_raw),
        HEAD,
    )

    steps, tokens, matrix, column, line = specs(PAIRS[0])
    inv, weight, trans, shift, cols, row_info, mine, other = pl.pallas_call(
        placed(prep_keys, PAIRS[0], heads, steps),
        grid=(steps,),
        in_specs=[tokens, tokens, pl.BlockSpec((heads, PAIRS[0] * C), lambda i: (0, i))],
        out_specs=[matrix] * 4 + [column, line] + [fixed(some, 2, C, C)] * 2,
        out_shape=[matrices] * 4 + [columns, lines, pair_maps, pair_maps],
        scratch_shapes=[carry, carry],
        name="prep_keys",
    )(key_raw, value_raw, log_decay)
    other = to_other_core(other)
    behind = from_chips_behind(small(placed(chip_maps), pair_maps, mine, other))

    steps, tokens, matrix, column, line = specs(PAIRS[1], reverse=True)
    inner, adjoint, norm_cols, norm_rows, mine_back, other_back = pl.pallas_call(
        placed(prep_queries, PAIRS[1], heads, steps),
        grid=(steps,),
        in_specs=[tokens] * 3
        + [fixed(1, width), fixed(group, blocks, C)]
        + [matrix, matrix, column, line],
        out_specs=[matrix, matrix, column, line] + [fixed(some, C, C)] * 2,
        out_shape=[matrices, matrices, columns, lines, pair_states, pair_states],
        scratch_shapes=[carry, line_scratch],
        name="prep_queries",
    )(query_raw, key_raw, out_grad, gain, squares, weight, trans, cols, row_info)
    other_back = to_other_core(other_back)
    stay, leave, back = small(
        placed(chip_states), [pair_states] * 3,
        mine, other, *behind, mine_back, other_back,
    )
    arrived = to_other_core(leave)
    ahead = from_chips_behind(back)

    steps, tokens, matrix, column, line = specs(PAIRS[2])
    scaled, fresh, starts, part = pl.pallas_call(
        placed(query_grads, PAIRS[2], heads, steps),
        grid=(steps,),
        in_specs=[tokens] * 4
        + [fixed(1, width), fixed(some, C, C), fixed(some, C, C)]
        + [matrix] * 4
        + [column, line, column],
        out_specs=[tokens, matrix, matrix, fixed(group, blocks, C)],
        out_shape=[shape((rows, width), f32), matrices, matrices, sums],
        scratch_shapes=[carry, line_scratch],
        name="query_grads",
    )(
        query_raw, key_raw, value_raw, out_grad, gain, stay, arrived,
        inv, weight, trans, shift, cols, row_info, norm_cols,
    )
    corrections = exchange(part, HEAD)

    stay, leave = small(
        placed(chip_adjoints, chips - 1), [pair_states] * 2,
        mine, other, *behind, *ahead, mine_back, other_back,
    )
    arrived = to_other_core(leave)

    def owned(array):
        return exchange(array.reshape(group, rows // group, array.shape[1]), HEAD)

    steps, tokens, matrix, column, line = specs(PAIRS[3])
    query_raw_grad = pl.pallas_call(
        functools.partial(finish_queries, PAIRS[3], heads),
        grid=(steps,),
        in_specs=[tokens, tokens, column, fixed(group, blocks, C)],
        out_specs=tokens,
        out_shape=shape((rows, width), bf16),
        scratch_shapes=[line_scratch],
        name="finish_queries",
    )(query_raw, scaled, norm_cols, corrections)
    first = owned(query_raw_grad)

    steps, tokens, matrix, column, line = specs(PAIRS[4], reverse=True)
    key_value = pl.pallas_call(
        placed(key_grads, PAIRS[4], heads),
        grid=(steps,),
        in_specs=[tokens] * 3
        + [fixed(1, width), fixed(some, C, C), fixed(some, C, C)]
        + [matrix] * 6
        + [column, line, line, pl.BlockSpec(memory_space=pl.ANY)],
        out_specs=pl.BlockSpec((PAIRS[4] * C, 2 * width), lambda i: (steps - 1 - i, 0)),
        out_shape=shape((rows, 2 * width), bf16),
        scratch_shapes=[carry],
        name="key_grads",
    )(
        query_raw, key_raw, out_grad, gain, stay, arrived,
        inv, trans, adjoint, inner, fresh, starts, cols, row_info, norm_rows, query_raw_grad,
    )
    second = owned(key_value)

    def lay(pieces):
        return pieces.transpose(1, 0, 2).reshape(rows // group, group * width)

    return lay(first), lay(second[:, :, :width]), lay(second[:, :, width:])


def solution(mesh):
    split = Mesh(mesh.devices.reshape(4, 2, 4, 4), ("seq_0", "seq_1", "head_0", "head_1"))
    return jax.shard_map(
        per_device,
        mesh=split,
        in_specs=(P(SEQ, HEAD), P(SEQ, HEAD), P(SEQ, HEAD), P(HEAD), P(HEAD, SEQ), P(SEQ, HEAD)),
        out_specs=(P(SEQ_HEAD, None), P(SEQ_HEAD, None), P(SEQ_HEAD, None)),
        check_vma=False,
    )
```

```python
import functools

import jax
import jax.numpy as jnp
from jax import lax
from jax.experimental import pallas as pl
from jax.experimental.pallas import tpu as pltpu
from jax.sharding import Mesh
from jax.sharding import PartitionSpec as P


D = 8192
C = 128
PAIRS = (8, 8, 2, 4, 2)
HEAD = ("head_0", "head_1")
SEQ = ("seq_0", "seq_1")
SEQ_HEAD = ("seq_0", "seq_1", "head_0", "head_1")
EPS = 1e-06
BASE = 16
SCALE = C ** (-0.5)

f32 = jnp.float32
bf16 = jnp.bfloat16


def halves(x):
    high = x.astype(bf16)
    return high, (x - high.astype(f32)).astype(bf16)


def nn(a, b):
    return lax.dot_general(a, b, (((1,), (0,)), ((), ())), preferred_element_type=f32)


def nt(a, b):
    return lax.dot_general(a, b, (((1,), (1,)), ((), ())), preferred_element_type=f32)


def mul3(form, a, b):
    left = jnp.concatenate(a, axis=1)
    blank = jnp.zeros_like(b[1])
    if form is nn:
        upper = jnp.concatenate([b[0], b[1]], axis=1)
        lower = jnp.concatenate([b[0], blank], axis=1)
    else:
        upper = jnp.concatenate([b[0], b[0]], axis=1)
        lower = jnp.concatenate([b[1], blank], axis=1)
    both = form(left, jnp.concatenate([upper, lower], axis=0))
    return both[:, :C] + both[:, C:]


def mul_left(form, a, b):
    return form(a[0], b) + form(a[1], b)


def mul_right(form, a, b):
    return form(a, b[0]) + form(a, b[1])


def iotas():
    return (
        lax.broadcasted_iota(jnp.int32, (C, C), 0),
        lax.broadcasted_iota(jnp.int32, (C, C), 1),
    )


def columns_of(rows):
    missing = C - rows.shape[0]
    return jnp.concatenate([rows, jnp.zeros((missing, C), f32)], axis=0).T


def tile(ref, b, h):
    return ref[b * C : (b + 1) * C, h * C : (h + 1) * C]


def square_sums(heads, query, out, lines):
    step = pl.program_id(0)
    blocks = query.shape[0] // C
    for b in range(blocks):
        total = jnp.zeros((C, C), f32)
        for h in range(heads):
            wide = tile(query, b, h).astype(f32)
            total += wide * wide
        lines[pl.ds(step * blocks + b, 1)] = jnp.sum(total.T, axis=0, keepdims=True)

    @pl.when(step == pl.num_programs(0) - 1)
    def _():
        out[...] = jnp.broadcast_to(lines[...][None], out.shape)


def placed(kernel, *settings):
    def run(*refs):
        kernel(*settings, (lax.axis_index("seq_0"), lax.axis_index("seq_1")), *refs)

    return run


def all_units(pair, heads):
    return [(b, h) for b in range(pair) for h in range(heads)]


def block_inverses(lower):
    row, col = iotas()
    inside = (row // BASE) == (col // BASE)
    packed = jnp.sum(jnp.where(inside, lower, 0.0).reshape(C // BASE, BASE, C), axis=0)
    place_row = lax.broadcasted_iota(jnp.int32, (BASE, C), 0)
    place_col = lax.broadcasted_iota(jnp.int32, (BASE, C), 1)
    result = jnp.where(place_row == place_col % BASE, 1.0, 0.0)
    for j in range(BASE - 1):
        entry = (place_col // BASE) * BASE + j
        factor = jnp.take_along_axis(packed, entry, axis=1, mode="promise_in_bounds")
        result = result - factor * result[j : j + 1]
    return jnp.where(inside, jnp.concatenate([result] * (C // BASE), axis=0), 0.0)


def after(early, late):
    step_map = halves(late[0])
    return (
        mul3(nn, step_map, halves(early[0])),
        mul3(nt, halves(early[1]), step_map) + late[1],
    )


def prep_keys(pair, heads, steps, place, key, value, decay, inv, weight, trans, shift, cols, rows, mine, other, whole, offset):
    step = pl.program_id(0)
    units = all_units(pair, heads)
    count = len(units)
    row, col = iotas()

    @pl.when(step == 0)
    def _():
        eye = jnp.where(row == col, 1.0, 0.0)
        for h in range(heads):
            whole[h] = eye
            offset[h] = jnp.zeros((C, C), f32)

    upto = jnp.where(row <= col, 1.0, 0.0)
    logs = jnp.concatenate([decay[:, b * C : (b + 1) * C] for b in range(pair)], axis=0)
    cumul_rows = jnp.dot(logs, upto, precision=lax.Precision.HIGHEST, preferred_element_type=f32)
    cumul_cols = columns_of(cumul_rows)

    raw = [tile(key, b, h) for b, h in units]
    scale_cols = []
    gathered = jnp.zeros((C, C), f32)
    for u in range(count):
        wide = raw[u].astype(f32)
        scale_cols.append(lax.rsqrt(jnp.sum(wide * wide, axis=1, keepdims=True) + EPS))
        gathered = jnp.where(col == u, scale_cols[u], gathered)
    scale_rows = gathered.T

    for b in range(pair):
        these = slice(b * heads, (b + 1) * heads)
        rows[b] = jnp.concatenate([cumul_rows[these], scale_rows[these]], axis=0)
        packed = jnp.zeros((C, C), f32)
        for h in range(heads):
            u = b * heads + h
            packed = jnp.where(col == h, cumul_cols[:, u : u + 1], packed)
            packed = jnp.where(col == heads + h, scale_cols[u], packed)
        cols[b * C : (b + 1) * C] = packed

    g_col = [cumul_cols[:, u : u + 1] for u in range(count)]
    g_row = [cumul_rows[u : u + 1] for u in range(count)]
    s_row = [scale_rows[u : u + 1] for u in range(count)]
    last = [g_row[u][:, C - 1 :] for u in range(count)]

    lower = []
    for u in range(count):
        gram = nt(raw[u], raw[u])
        decayed = jnp.exp(jnp.where(row > col, g_col[u] - g_row[u], 0.0))
        lower.append(
            jnp.where(row > col, 2.0 * decayed * (scale_cols[u] * s_row[u]) * gram, 0.0)
        )

    apart = row ^ col
    result = [block_inverses(lower[u]) for u in range(count)]
    size = BASE
    while size < C:
        here = (apart >= size) & (apart < 2 * size)
        split = [halves(x) for x in result]
        below = [halves(jnp.where(here, lower[u], 0.0)) for u in range(count)]
        inner = [halves(mul3(nn, below[u], split[u])) for u in range(count)]
        result = [result[u] - mul3(nn, split[u], inner[u]) for u in range(count)]
        size *= 2

    split = [halves(x) for x in result]
    scaled, moved = [], []
    for u, (b, h) in enumerate(units):
        inv[b, h] = result[u]
        end = jnp.exp(last[u] - g_row[u])
        turned = tile(value, b, h).T
        amount = mul_right(nt, turned, split[u]) * (2.0 * end * s_row[u])
        moved.append(mul_left(nn, halves(amount), raw[u]))
        shift[b, h] = moved[u]
        start = jnp.exp(g_row[u]) * s_row[u]
        scaled.append(mul_left(nn, halves(result[u] * start), raw[u]))
        weight[b, h] = scaled[u]
    maps = []
    for u, (b, h) in enumerate(units):
        end = jnp.exp(last[u] - g_col[u]) * (2.0 * scale_cols[u])
        drop = mul_right(nn, raw[u].T, halves(scaled[u] * end))
        maps.append(jnp.where(row == col, jnp.exp(last[u]), 0.0) - drop)
        trans[b, h] = maps[u]

    runs = [[(maps[b * heads + h], moved[b * heads + h]) for h in range(heads)] for b in range(pair)]
    while len(runs) > 1:
        runs = [
            [after(early, late) for early, late in zip(runs[i], runs[i + 1])]
            for i in range(0, len(runs), 2)
        ]
    for h in range(heads):
        whole[h], offset[h] = after((whole[h], offset[h]), runs[0][h])

    @pl.when(step == steps - 1)
    def _():
        half = heads // 2
        first = place[1] * half
        for j in range(half):
            mine[j, 0] = whole[first + j]
            mine[j, 1] = offset[first + j]
            other[j, 0] = whole[half - first + j]
            other[j, 1] = offset[half - first + j]


def chip_maps(place, mine, other, out):
    first = place[1] == 0
    for j in range(mine.shape[0]):
        early = [jnp.where(first, mine[j, i], other[j, i]) for i in range(2)]
        late = [jnp.where(first, other[j, i], mine[j, i]) for i in range(2)]
        out[j, 0], out[j, 1] = after(early, late)


def chip_states(place, mine, other, one, two, three, mine_back, other_back, stay, leave, back):
    first = place[1] == 0
    for j in range(mine.shape[0]):
        state = jnp.where(place[0] >= 3, three[j, 1], 0.0)
        for k, behind in ((2, two), (1, one)):
            moved = mul3(nt, halves(state), halves(behind[j, 0])) + behind[j, 1]
            state = jnp.where(place[0] >= k, moved, state)
        early = [jnp.where(first, mine[j, i], other[j, i]) for i in range(2)]
        step_map = halves(early[0])
        after = mul3(nt, halves(state), step_map) + early[1]
        stay[j] = jnp.where(first, state, after)
        leave[j] = jnp.where(first, after, state)
        early_back = jnp.where(first, mine_back[j], other_back[j])
        late_back = jnp.where(first, other_back[j], mine_back[j])
        back[j] = mul3(nn, halves(late_back), step_map) + early_back


def chip_adjoints(last, place, mine, other, one, two, three, one_back, two_back, three_back, mine_back, other_back, stay, leave):
    first = place[1] == 0
    for j in range(mine.shape[0]):
        state = jnp.where(place[0] + 3 <= last, one_back[j], 0.0)
        for k, ahead, term in ((2, two, two_back), (1, three, three_back)):
            moved = mul3(nn, halves(state), halves(ahead[j, 0])) + term[j]
            state = jnp.where(place[0] + k <= last, moved, state)
        late = jnp.where(first, other[j, 0], mine[j, 0])
        late_back = jnp.where(first, other_back[j], mine_back[j])
        before = mul3(nn, halves(state), halves(late)) + late_back
        stay[j] = jnp.where(first, before, state)
        leave[j] = jnp.where(first, state, before)


def prep_queries(pair, heads, steps, place, query, key, grad, gain, sums, weight, trans, cols, rows, inner, adjoint, norm_cols, norm_rows, mine, other, total, norms):
    step = pl.program_id(0)
    units = all_units(pair, heads)
    count = len(units)
    row, col = iotas()

    @pl.when(step == 0)
    def _():
        for h in range(heads):
            total[h] = jnp.zeros((C, C), f32)
        norms[...] = lax.rsqrt(jnp.sum(sums[...], axis=0) * (1.0 / D) + EPS)

    first = (steps - 1 - step) * pair
    n_rows = [norms[pl.ds(first + b, 1)] for b in range(pair)]
    n_cols = columns_of(jnp.concatenate(n_rows, axis=0))
    for b in range(pair):
        norm_rows[b] = jnp.broadcast_to(n_rows[b], (8, C))
        norm_cols[b * C : (b + 1) * C] = jnp.broadcast_to(n_cols[:, b : b + 1], (C, C))

    scaled_query, mixing = [], []
    for u, (b, h) in enumerate(units):
        here = cols[b * C : (b + 1) * C]
        g_col = here[:, h : h + 1]
        g_row = rows[b, h : h + 1]
        s_row = rows[b, heads + h : heads + h + 1]
        n_col = n_cols[:, b : b + 1]
        wide = tile(query, b, h).astype(f32) * (gain[:, h * C : (h + 1) * C] * SCALE)
        decayed = jnp.exp(jnp.where(row >= col, g_col - g_row, 0.0))
        scores = mul_left(nt, halves(wide), tile(key, b, h))
        mixing.append(
            halves(jnp.where(row >= col, 2.0 * decayed * (n_col * s_row) * scores, 0.0))
        )
        scaled_query.append(halves(wide * (jnp.exp(g_col) * n_col)))
    turned = [tile(grad, b, h).T for b, h in units]
    mixed = [mul_right(nn, turned[u], mixing[u]) for u in range(count)]
    terms = []
    for u, (b, h) in enumerate(units):
        inner[b, h] = mixed[u]
        terms.append(
            mul_right(nn, turned[u], scaled_query[u])
            - mul3(nn, halves(mixed[u]), halves(weight[b, h]))
        )
        adjoint[b, h] = terms[u]
    for b in reversed(range(pair)):
        for h in range(heads):
            u = b * heads + h
            total[h] = mul3(nn, halves(total[h]), halves(trans[b, h])) + terms[u]

    @pl.when(step == steps - 1)
    def _():
        half = heads // 2
        begin = place[1] * half
        for j in range(half):
            mine[j] = total[begin + j]
            other[j] = total[half - begin + j]


def query_grads(pair, heads, steps, place, query, key, value, grad, gain, mine, other, inv, weight, trans, shift, cols, rows, norm_cols, scaled, fresh, starts, part, state, sums_so_far):
    step = pl.program_id(0)
    units = all_units(pair, heads)
    row, col = iotas()

    @pl.when(step == 0)
    def _():
        half = heads // 2
        first = place[1] * half
        for j in range(half):
            state[first + j] = mine[j]
            state[half - first + j] = other[j]

    for b in range(pair):
        for h in range(heads):
            starts[b, h] = state[h]
            state[h] = mul3(nt, halves(state[h]), halves(trans[b, h])) + shift[b, h]
    begin = [halves(starts[b, h]) for b, h in units]
    amounts = []
    for u, (b, h) in enumerate(units):
        amount = mul_left(nn, halves(inv[b, h]), tile(value, b, h)) - mul3(
            nt, halves(weight[b, h]), begin[u]
        )
        fresh[b, h] = amount
        amounts.append(halves(amount))
    cross = [mul_right(nt, tile(grad, b, h), amounts[u]) for u, (b, h) in enumerate(units)]
    sums = [jnp.zeros((C, 1), f32) for _ in range(pair)]
    for u, (b, h) in enumerate(units):
        here = cols[b * C : (b + 1) * C]
        g_col = here[:, h : h + 1]
        g_row = rows[b, h : h + 1]
        s_row = rows[b, heads + h : heads + h + 1]
        decayed = jnp.exp(jnp.where(row >= col, g_col - g_row, 0.0))
        mixed = jnp.where(row >= col, 2.0 * decayed * s_row * cross[u], 0.0)
        result = mul_left(nn, halves(mixed), tile(key, b, h)) + jnp.exp(g_col) * mul_right(
            nn, tile(grad, b, h), begin[u]
        )
        result = result * (gain[:, h * C : (h + 1) * C] * SCALE)
        scaled[b * C : (b + 1) * C, h * C : (h + 1) * C] = result
        sums[b] = sums[b] + jnp.sum(result * tile(query, b, h).astype(f32), axis=1, keepdims=True)
    for b in range(pair):
        full = sums[b] * norm_cols[b * C : (b + 1) * C]
        sums_so_far[pl.ds(step * pair + b, 1)] = full.T[:1]

    @pl.when(step == steps - 1)
    def _():
        part[...] = jnp.broadcast_to(sums_so_far[...][None], part.shape)


def finish_queries(pair, heads, query, scaled, norm_cols, sums, out, corrections):
    step = pl.program_id(0)

    @pl.when(step == 0)
    def _():
        corrections[...] = jnp.sum(sums[...], axis=0) * (1.0 / D)

    lines = [corrections[pl.ds(step * pair + b, 1)] for b in range(pair)]
    columns = columns_of(jnp.concatenate(lines, axis=0))
    for b in range(pair):
        part = slice(b * C, (b + 1) * C)
        norm = norm_cols[part]
        factor = norm * norm * columns[:, b : b + 1]
        for h in range(heads):
            side = slice(h * C, (h + 1) * C)
            out[part, side] = (
                norm * scaled[part, side] - query[part, side].astype(f32) * factor
            ).astype(bf16)


def key_grads(pair, heads, place, query, key, grad, gain, mine, other, inv, trans, adjoint, inner, fresh, starts, cols, rows, norm_rows, ready, out, state):
    step = pl.program_id(0)
    units = all_units(pair, heads)
    count = len(units)
    row, col = iotas()
    width = heads * C

    @pl.when(step == 0)
    def _():
        half = heads // 2
        first = place[1] * half
        for j in range(half):
            state[first + j] = mine[j]
            state[half - first + j] = other[j]

    ends = [None] * count
    for b in reversed(range(pair)):
        for h in range(heads):
            u = b * heads + h
            ends[u] = halves(state[h])
            state[h] = mul3(nn, ends[u], halves(trans[b, h])) + adjoint[b, h]
    g_row = [rows[b, h : h + 1] for b, h in units]
    s_row = [rows[b, heads + h : heads + h + 1] for b, h in units]
    keys = [tile(key, b, h) for b, h in units]
    amounts = [halves(fresh[b, h]) for b, h in units]
    turned = []
    for u, (b, h) in enumerate(units):
        end = jnp.exp(g_row[u][:, C - 1 :] - g_row[u]) * (2.0 * s_row[u])
        turned.append(halves(inner[b, h] + mul_left(nt, ends[u], keys[u]) * end))
    results = [mul3(nn, turned[u], halves(inv[b, h])).T for u, (b, h) in enumerate(units)]
    for u, (b, h) in enumerate(units):
        out[b * C : (b + 1) * C, width + h * C : width + (h + 1) * C] = results[u].astype(bf16)
    results = [halves(x) for x in results]
    against = [mul3(nt, results[u], amounts[u]) for u in range(count)]
    across = [mul_left(nt, amounts[u], tile(grad, b, h)) for u, (b, h) in enumerate(units)]
    for u, (b, h) in enumerate(units):
        here = cols[b * C : (b + 1) * C]
        g_col = here[:, h : h + 1]
        s_col = here[:, heads + h : heads + h + 1]
        n_row = norm_rows[b, :1]
        below = jnp.exp(jnp.where(row > col, g_col - g_row[u], 0.0))
        pulled = jnp.where(row > col, -2.0 * below * against[u], 0.0)
        both = (pulled + pulled.T) * s_row[u]
        above = jnp.exp(jnp.where(row <= col, g_row[u] - g_col, 0.0))
        mixed = jnp.where(row <= col, 2.0 * above * n_row * across[u], 0.0)
        total = mul_left(nn, halves(both), keys[u])
        total += mul_left(nn, halves(mixed), tile(query, b, h)) * (
            gain[:, h * C : (h + 1) * C] * SCALE
        )
        total -= jnp.exp(g_col) * mul3(nn, results[u], halves(starts[b, h]))
        end = 2.0 * jnp.exp(g_row[u][:, C - 1 :] - g_col)
        total += end * mul3(nn, amounts[u], ends[u])
        unit = keys[u].astype(f32) * s_col
        along = jnp.sum(unit * total, axis=1, keepdims=True)
        out[b * C : (b + 1) * C, h * C : (h + 1) * C] = (
            s_col * (total - unit * along)
        ).astype(bf16)


def per_device(query_raw, key_raw, value_raw, query_gain, log_decay, out_grad):
    rows, width = query_raw.shape
    heads = log_decay.shape[0]
    blocks = rows // C
    group = lax.axis_size(HEAD)
    gain = query_gain.reshape(1, width)
    shape = jax.ShapeDtypeStruct

    def specs(pair, reverse=False):
        steps = blocks // pair

        def at(i):
            return steps - 1 - i if reverse else i

        return (
            steps,
            pl.BlockSpec((pair * C, width), lambda i: (at(i), 0)),
            pl.BlockSpec((pair, heads, C, C), lambda i: (at(i), 0, 0, 0)),
            pl.BlockSpec((pair * C, C), lambda i: (at(i), 0)),
            pl.BlockSpec((pair, 8, C), lambda i: (at(i), 0, 0)),
        )

    def fixed(*block):
        return pl.BlockSpec(block, lambda i: (0,) * len(block))

    def exchange(value, axis):
        return lax.all_to_all(value, axis, 0, 0, tiled=True)

    matrices = shape((blocks, heads, C, C), f32)
    columns = shape((rows, C), f32)
    lines = shape((blocks, 8, C), f32)
    sums = shape((group, blocks, C), f32)
    carry = pltpu.VMEM((heads, C, C), f32)
    line_scratch = pltpu.VMEM((blocks, C), f32)

    cores = lax.axis_size("seq_1")
    chips = lax.axis_size("seq_0")
    assert (chips, cores) == (4, 2) and heads % 2 == 0
    some = heads // 2
    pair_maps = shape((some, 2, C, C), f32)
    pair_states = shape((some, C, C), f32)

    def to_other_core(value):
        return lax.ppermute(value, "seq_1", [(0, 1), (1, 0)])

    def from_chips_behind(value):
        pieces = []
        for k in range(1, chips):
            pieces.append(
                lax.ppermute(value, "seq_0", [(i, (i + k) % chips) for i in range(chips)])
            )
        return pieces

    def small(kernel, out_shape, *operands):
        return pl.pallas_call(
            kernel,
            in_specs=[pl.BlockSpec(memory_space=pltpu.VMEM)] * len(operands),
            out_shape=out_shape,
        )(*operands)

    squares = exchange(
        pl.pallas_call(
            functools.partial(square_sums, heads),
            grid=(2,),
            in_specs=[pl.BlockSpec((rows // 2, width), lambda i: (i, 0))],
            out_specs=fixed(group, blocks, C),
            out_shape=sums,
            scratch_shapes=[line_scratch],
            name="square_sums",
        )(query_raw),
        HEAD,
    )

    steps, tokens, matrix, column, line = specs(PAIRS[0])
    inv, weight, trans, shift, cols, row_info, mine, other = pl.pallas_call(
        placed(prep_keys, PAIRS[0], heads, steps),
        grid=(steps,),
        in_specs=[tokens, tokens, pl.BlockSpec((heads, PAIRS[0] * C), lambda i: (0, i))],
        out_specs=[matrix] * 4 + [column, line] + [fixed(some, 2, C, C)] * 2,
        out_shape=[matrices] * 4 + [columns, lines, pair_maps, pair_maps],
        scratch_shapes=[carry, carry],
        name="prep_keys",
    )(key_raw, value_raw, log_decay)
    other = to_other_core(other)
    behind = from_chips_behind(small(placed(chip_maps), pair_maps, mine, other))

    steps, tokens, matrix, column, line = specs(PAIRS[1], reverse=True)
    inner, adjoint, norm_cols, norm_rows, mine_back, other_back = pl.pallas_call(
        placed(prep_queries, PAIRS[1], heads, steps),
        grid=(steps,),
        in_specs=[tokens] * 3
        + [fixed(1, width), fixed(group, blocks, C)]
        + [matrix, matrix, column, line],
        out_specs=[matrix, matrix, column, line] + [fixed(some, C, C)] * 2,
        out_shape=[matrices, matrices, columns, lines, pair_states, pair_states],
        scratch_shapes=[carry, line_scratch],
        name="prep_queries",
    )(query_raw, key_raw, out_grad, gain, squares, weight, trans, cols, row_info)
    other_back = to_other_core(other_back)
    stay, leave, back = small(
        placed(chip_states), [pair_states] * 3,
        mine, other, *behind, mine_back, other_back,
    )
    arrived = to_other_core(leave)
    ahead = from_chips_behind(back)

    steps, tokens, matrix, column, line = specs(PAIRS[2])
    scaled, fresh, starts, part = pl.pallas_call(
        placed(query_grads, PAIRS[2], heads, steps),
        grid=(steps,),
        in_specs=[tokens] * 4
        + [fixed(1, width), fixed(some, C, C), fixed(some, C, C)]
        + [matrix] * 4
        + [column, line, column],
        out_specs=[tokens, matrix, matrix, fixed(group, blocks, C)],
        out_shape=[shape((rows, width), f32), matrices, matrices, sums],
        scratch_shapes=[carry, line_scratch],
        name="query_grads",
    )(
        query_raw, key_raw, value_raw, out_grad, gain, stay, arrived,
        inv, weight, trans, shift, cols, row_info, norm_cols,
    )
    corrections = exchange(part, HEAD)

    stay, leave = small(
        placed(chip_adjoints, chips - 1), [pair_states] * 2,
        mine, other, *behind, *ahead, mine_back, other_back,
    )
    arrived = to_other_core(leave)

    def owned(array):
        return exchange(array.reshape(group, rows // group, array.shape[1]), HEAD)

    steps, tokens, matrix, column, line = specs(PAIRS[3])
    query_raw_grad = pl.pallas_call(
        functools.partial(finish_queries, PAIRS[3], heads),
        grid=(steps,),
        in_specs=[tokens, tokens, column, fixed(group, blocks, C)],
        out_specs=tokens,
        out_shape=shape((rows, width), bf16),
        scratch_shapes=[line_scratch],
        name="finish_queries",
    )(query_raw, scaled, norm_cols, corrections)
    first = owned(query_raw_grad)

    steps, tokens, matrix, column, line = specs(PAIRS[4], reverse=True)
    key_value = pl.pallas_call(
        placed(key_grads, PAIRS[4], heads),
        grid=(steps,),
        in_specs=[tokens] * 3
        + [fixed(1, width), fixed(some, C, C), fixed(some, C, C)]
        + [matrix] * 6
        + [column, line, line, pl.BlockSpec(memory_space=pl.ANY)],
        out_specs=pl.BlockSpec((PAIRS[4] * C, 2 * width), lambda i: (steps - 1 - i, 0)),
        out_shape=shape((rows, 2 * width), bf16),
        scratch_shapes=[carry],
        name="key_grads",
    )(
        query_raw, key_raw, out_grad, gain, stay, arrived,
        inv, trans, adjoint, inner, fresh, starts, cols, row_info, norm_rows, query_raw_grad,
    )
    second = owned(key_value)

    def lay(pieces):
        return pieces.transpose(1, 0, 2).reshape(rows // group, group * width)

    return lay(first), lay(second[:, :, :width]), lay(second[:, :, width:])


def solution(mesh):
    split = Mesh(mesh.devices.reshape(4, 2, 4, 4), ("seq_0", "seq_1", "head_0", "head_1"))
    return jax.shard_map(
        per_device,
        mesh=split,
        in_specs=(P(SEQ, HEAD), P(SEQ, HEAD), P(SEQ, HEAD), P(HEAD), P(HEAD, SEQ), P(SEQ, HEAD)),
        out_specs=(P(SEQ_HEAD, None), P(SEQ_HEAD, None), P(SEQ_HEAD, None)),
        check_vma=False,
    )
```
